32 devices in a mesh: group: 8 (over z, y), lat: 2 (over x), rad: 2 (over core).
Axes of the slice: x: 2, y: 2, z: 4, core: 2. Of those that a mesh axis runs over, the one named last changes fastest.
Arguments:
- displacement_prev: float32 [3, 4, 128, 256], P(None, 'rad', 'group', 'lat'), may hold values from -2.5 to 2.5
- shear_modulus: float32 [4, 128, 256], P('rad', 'group', 'lat'), may hold values from 1 to 10
- viscosity: float32 [4, 128, 256], P('rad', 'group', 'lat'), may hold values from 0.5 to 20
- element_matrix: float32 [24, 24], replicated, as said below
- regrid_index: int32 [128, 2, 4], P('group', 'lat'), may hold values from 0 to 63
- regrid_weight: float32 [128, 2, 4], P('group', 'lat'), may hold values from 0.1 to 0.6
- ice_thickness: float32 [32, 256], P('lat'), may hold values from 0.5 to 4
- bed_elevation: float32 [32, 256], P('lat'), may hold values from -3 to 3
- basal_friction: float32 [32, 256], P('lat'), may hold values from 0.2 to 5
- ice_mask: int32 [32, 256], P('lat'), may hold values 0 or 1
- speed_guess: float32 [16, 32, 256], P(None, 'lat'), may hold values from -3 to 3
Outputs:
- displacement: float32 [3, 4, 128, 256], P(None, 'rad', 'group', 'lat')
- bed_new: float32 [32, 256], P('lat')
The draws below stay inside these ranges and needn't reach their ends.
Inputs may be any that keep to these rules, and one draw needn't show every extreme that they name: `regrid_index`: names a block of the ice map: block b is row b // 2, columns 128 * (b % 2) to 128 * (b % 2) + 127. `element_matrix`: symmetric positive definite.
All inputs are finite; a program needn't handle non-finite values. No bound on the sum of `ice_mask` on one device may be relied on, other than what follows from the above.
Results may differ from the reference program's by a relative error of at most 0.0019.
Values may be sent and summed in bfloat16 or wider, within the bound.
No kernel may reach another device: no remote copies, remote signals or barrier semaphores. Data moves between devices by JAX's collectives and lax.ppermute only.
A program may use at most 64 MiB of HBM per device.

```python
import math
import jax
import jax.numpy as jnp
from jax import lax

LA = 16
BLOCK = 128
NL = 16
KB = 4
SWEEPS = 6
ITERS = 4
NR = 4
NA = 128
NB = 256
NIR = 32
MAPW = 256
NIB = 64
N_LAT = 2


def draw_element_matrix(key, part):
    noise_key, diag_key = jax.random.split(jax.random.fold_in(key, 11))
    noise_part = 0.2 * jax.random.normal(noise_key, (24, 24), jnp.float32)
    off_mask = 1.0 - jnp.eye(24, dtype=jnp.float32)
    symmetric = 0.5 * (noise_part + noise_part.T) * off_mask
    spread = jax.random.uniform(diag_key, (24,), jnp.float32, 1.0, 2.0)
    return symmetric + jnp.diag(jnp.sum(jnp.abs(symmetric), 1) + spread)


def plant(entries, rng, low, largest):
    longest = entries.shape.index(max(entries.shape))
    spots = []
    for shift in (0, 1):
        where = [jax.random.randint(jax.random.fold_in(rng, axis), (), 0, length) for axis, length in enumerate(entries.shape)]
        where[longest] = (where[longest] + shift) % entries.shape[longest]
        spots.append(tuple(where))
    return entries.at[spots[0]].set(low).at[spots[1]].set(largest)


def shard_levels(own_key, extent, shards, smallest, high):
    loudness, own = 1.0, jax.random.fold_in(own_key, 6)
    for axis_at, parts in shards:
        draws = jnp.exp(jax.random.uniform(jax.random.fold_in(own, axis_at), (parts,), jnp.float32, smallest / len(shards), high / len(shards)))
        loudness = loudness * jnp.repeat(draws, extent[axis_at] // parts).reshape([-1 if axis == axis_at else 1 for axis in range(len(extent))])
    return loudness


def noise(key, shape, scale, reach, cuts=(), kind=jnp.bfloat16):
    level = shard_levels(key, shape, cuts, -0.22, 0.18) if cuts else 1.0
    drawn = jax.random.normal(key, shape, jnp.float32) * scale * level
    return jnp.minimum(jnp.maximum(drawn, -reach), reach).astype(kind)


def setup_inputs(seed: int = 0) -> dict:
    seeds = jax.random.split(jax.random.key(seed), 12)
    displacement_prev = noise(seeds[0], (3, NR, NA, NB), 0.3, 2.5, ((1, 2), (2, 8), (3, 2)), jnp.float32)
    shear_modulus = jnp.clip(jnp.exp(math.log(10.0) - 2.3025851 * jax.random.uniform(seeds[1], (NR, NA, NB), jnp.float32) ** shard_levels(seeds[1], (NR, NA, NB), ((0, 2), (1, 8), (2, 2)), -0.2, 0.2)), 1.0, 10.0)
    viscosity = jnp.clip(jnp.exp(math.log(20.0) - 3.6888795 * jax.random.uniform(seeds[2], (NR, NA, NB), jnp.float32) ** shard_levels(seeds[2], (NR, NA, NB), ((0, 2), (1, 8), (2, 2)), -0.2, 0.2)), 0.5, 20.0)
    element_matrix = draw_element_matrix(jax.random.fold_in(seeds[11], 71), 0)
    regrid_index = plant(jax.random.randint(seeds[4], (NA, N_LAT, KB), 0, NIB), jax.random.fold_in(seeds[4], 1), 0, NIB - 1).astype(jnp.int32)
    regrid_weight = jnp.clip(0.1 + 0.5 * jax.random.uniform(seeds[5], (NA, N_LAT, KB), jnp.float32) ** shard_levels(seeds[5], (NA, N_LAT, KB), ((0, 8), (1, 2)), -0.2, 0.2), 0.1, 0.6)
    ice_thickness = jnp.clip(jnp.exp(math.log(4.0) - 2.0794415 * jax.random.uniform(seeds[6], (NIR, MAPW), jnp.float32) ** shard_levels(seeds[6], (NIR, MAPW), ((0, 2),), -0.2, 0.2)), 0.5, 4.0)
    bed_elevation = noise(seeds[7], (NIR, MAPW), 0.5, 3.0, ((0, 2),), jnp.float32)
    basal_friction = jnp.clip(jnp.exp(math.log(5.0) - 3.218876 * jax.random.uniform(seeds[8], (NIR, MAPW), jnp.float32) ** shard_levels(seeds[8], (NIR, MAPW), ((0, 2),), -0.2, 0.2)), 0.2, 5.0)
    ice_mask = plant((jax.random.randint(seeds[9], (NIR, MAPW), 0, 4) < 3).astype(jnp.int32), jax.random.fold_in(seeds[9], 1), 0, 1)
    speed_guess = noise(seeds[10], (NL, NIR, MAPW), 0.5, 3.0, ((1, 2),), jnp.float32)
    return {"displacement_prev": displacement_prev, "shear_modulus": shear_modulus, "viscosity": viscosity, "element_matrix": element_matrix, "regrid_index": regrid_index, "regrid_weight": regrid_weight, "ice_thickness": ice_thickness, "bed_elevation": bed_elevation, "basal_friction": basal_friction, "ice_mask": ice_mask, "speed_guess": speed_guess}


LOAD_SCALE = 20.0
UPLIFT_SCALE = 0.5
TIME_SCALE = 1.0
ICE_STEP = 0.5
ASPECT = 0.01
STRAIN_FLOOR = 0.01
CORNERS = [(layer_bit, row_bit, col_bit) for layer_bit in (0, 1) for row_bit in (0, 1) for col_bit in (0, 1)]


def corner_mean(padded_coef, layer_count, col_count, depth_count):
    summed = jnp.zeros((layer_count, col_count, depth_count), padded_coef.dtype)
    for layer_bit, row_bit, col_bit in CORNERS:
        summed = summed + padded_coef[layer_bit:layer_bit + layer_count, row_bit:row_bit + col_count, col_bit:col_bit + depth_count]
    return summed / 8.0


def element_forces(padded_field, padded_coef, kernel, layer_id):
    field_slab = lax.dynamic_slice_in_dim(padded_field, layer_id, 2, 1)
    coef_slab = lax.dynamic_slice_in_dim(padded_coef, layer_id, 2, 0)
    col_count = field_slab.shape[2] - 1
    depth_count = field_slab.shape[3] - 1
    pieces = [field_slab[:, layer_bit, row_bit:row_bit + col_count, col_bit:col_bit + depth_count] for layer_bit, row_bit, col_bit in CORNERS]
    stacked = jnp.concatenate(pieces, 0)
    weight_mean = corner_mean(coef_slab, 1, col_count, depth_count)[0]
    return jnp.einsum("pq,qab->pab", kernel, stacked, precision=lax.Precision.HIGHEST) * weight_mean


def apply_operator(node_field, node_coef, kernel, domain):
    padded_field = jnp.pad(node_field, ((0, 0), (1, 1), (1, 1), (1, 1)))
    padded_coef = jnp.pad(node_coef, 1)
    col_count = node_field.shape[2]
    depth_count = node_field.shape[3]

    def node_layer(layer_id):
        below_layer = element_forces(padded_field, padded_coef, kernel, layer_id)
        above_layer = element_forces(padded_field, padded_coef, kernel, layer_id + 1)
        summed = jnp.zeros((3, col_count, depth_count), padded_field.dtype)
        for corner_id, (layer_bit, row_bit, col_bit) in enumerate(CORNERS):
            source = above_layer if layer_bit == 0 else below_layer
            summed = summed + source[3 * corner_id:3 * corner_id + 3, 1 - row_bit:1 - row_bit + col_count, 1 - col_bit:1 - col_bit + depth_count]
        return summed

    layers = lax.map(node_layer, jnp.arange(node_field.shape[1], dtype=jnp.int32))
    return jnp.transpose(layers, (1, 0, 2, 3)) * domain


def pad_rows(values):
    widths = [(0, 0)] * (values.ndim - 2) + [(1, 1), (0, 0)]
    return jnp.pad(values, widths)


def column_neighbours(values):
    zero_col = jnp.zeros_like(values[..., :1])
    east_side = jnp.concatenate([values[..., 1:], zero_col], -1)
    west_side = jnp.concatenate([zero_col, values[..., :-1]], -1)
    return east_side, west_side


def ice_sweep(velocity, padded_speed, thickness, friction, driving):
    levels = velocity.shape[0]
    north_side = padded_speed[:, 2:, :]
    south_side = padded_speed[:, :-2, :]
    east_side, west_side = column_neighbours(velocity)
    inverse = (levels - 1) / thickness
    slope_rows = 0.5 * (north_side - south_side)
    slope_cols = 0.5 * (east_side - west_side)
    slope_levels = jnp.concatenate([velocity[1:2] - velocity[0:1], 0.5 * (velocity[2:] - velocity[:-2]), velocity[-1:] - velocity[-2:-1]], 0) * inverse
    strain = slope_rows ** 2 + 0.25 * slope_cols ** 2 + 0.25 * slope_levels ** 2 + STRAIN_FLOOR
    stiffness = 0.5 * strain ** (-1.0 / 3.0)
    vertical = ASPECT * inverse ** 2 * 0.5 * (stiffness[1:] + stiffness[:-1])
    neighbours = stiffness * (north_side + south_side + east_side + west_side)
    factors = []
    upper_prev = None
    values_prev = None
    for level_id in range(levels):
        diagonal = 4.0 * stiffness[level_id]
        if level_id > 0:
            diagonal = diagonal + vertical[level_id - 1]
        if level_id < levels - 1:
            diagonal = diagonal + vertical[level_id]
        if level_id == 0:
            diagonal = diagonal + friction
        right_side = driving + neighbours[level_id]
        if level_id > 0:
            lower_coef = -vertical[level_id - 1]
            diagonal = diagonal - lower_coef * upper_prev
            right_side = right_side - lower_coef * values_prev
        upper_prev = (-vertical[level_id] / diagonal) if level_id < levels - 1 else None
        values_prev = right_side / diagonal
        factors.append((upper_prev, values_prev))
    solution = [None] * levels
    solution[levels - 1] = factors[levels - 1][1]
    for level_id in range(levels - 2, -1, -1):
        solution[level_id] = factors[level_id][1] - factors[level_id][0] * solution[level_id + 1]
    return jnp.stack(solution, 0)


def reference(displacement_prev, shear_modulus, viscosity, element_matrix, regrid_index, regrid_weight, ice_thickness, bed_elevation, basal_friction, ice_mask, speed_guess):
    ice_present = ice_mask.astype(jnp.float32)
    surface = bed_elevation + ice_thickness
    padded_surface = pad_rows(surface)
    driving = -ice_present * ice_thickness * 0.5 * (padded_surface[2:] - padded_surface[:-2])
    velocity = speed_guess
    for sweep_id in range(SWEEPS):
        velocity = ice_sweep(velocity, pad_rows(velocity), ice_thickness, basal_friction, driving)
    ice_flux = ice_thickness * jnp.mean(velocity, 0)
    padded_flux = pad_rows(ice_flux)
    new_thickness = ice_thickness - ICE_STEP * 0.5 * (padded_flux[2:] - padded_flux[:-2])
    ice_load = (ice_present * new_thickness).astype(jnp.bfloat16)
    blocks = ice_load.astype(jnp.float32).reshape(NIB, BLOCK)
    picked = jnp.take(blocks, regrid_index.reshape(-1), axis=0).reshape(NA, N_LAT, KB, BLOCK)
    surface_thickness = jnp.sum(regrid_weight[..., None] * picked, 2).reshape(NA, NB)
    rows_index = jnp.arange(NA, dtype=jnp.int32)
    domain = (rows_index < NA - LA).astype(jnp.float32)[None, None, :, None]
    relax_ratio = TIME_SCALE * shear_modulus / viscosity
    modulus = domain[0] * shear_modulus / (1.0 + relax_ratio)
    relaxed = modulus * relax_ratio / (1.0 + relax_ratio)
    load_field = jnp.zeros(displacement_prev.shape, jnp.float32).at[2, 0].set(-LOAD_SCALE * surface_thickness * domain[0, 0])
    solution = displacement_prev * domain
    residual = load_field - apply_operator(solution, relaxed, element_matrix, domain)
    direction = residual
    norm_now = jnp.sum(residual * residual)
    for iter_id in range(ITERS):
        mapped = apply_operator(direction, modulus, element_matrix, domain)
        step_size = norm_now / jnp.sum(direction * mapped)
        solution = solution + step_size * direction
        residual = residual - step_size * mapped
        norm_next = jnp.sum(residual * residual)
        direction = residual + (norm_next / norm_now) * direction
        norm_now = norm_next
    column_lift = jnp.mean(solution[2], 0)
    surface_lift = column_lift.reshape(NA, N_LAT, 1, BLOCK) * regrid_weight[..., None]
    uplift = jax.ops.segment_sum(surface_lift.reshape(-1, BLOCK), regrid_index.reshape(-1), num_segments=NIB)
    bed_new = bed_elevation + UPLIFT_SCALE * uplift.reshape(NIR, MAPW)
    return solution, bed_new
```

```python
import functools

import jax
import jax.numpy as jnp
import numpy as np
from jax import lax
from jax.experimental import pallas as pl
from jax.experimental.pallas import tpu as pltpu
from jax.sharding import PartitionSpec as P

SWEEPS = 6
ITERS = 4
HALO = 8
COMPS = 3
LAYERS = 4
PAIR = 2 * LAYERS
VEC = COMPS * PAIR
LOAD_SCALE = 20.0
UPLIFT_SCALE = 0.5
ASPECT = 0.01
STRAIN_FLOOR = 0.01
TYPICAL_MODULUS = 2.2

F32 = jnp.float32
BF16 = jnp.bfloat16


def vmem():
    return pl.BlockSpec(memory_space=pltpu.VMEM)


def iota(shape, dim):
    return lax.broadcasted_iota(jnp.int32, shape, dim)


def shift_lanes(x, step):
    size = x.shape[1]
    lanes = iota(x.shape, 1)
    edge = size - 1 if step == 1 else 0
    return jnp.where(lanes == edge, 0.0, pltpu.roll(x, size - 1 if step == 1 else 1, 1))


def ice_kernel(*refs, masked):
    if masked:
        speed, thick, bed, fric, mask, before, after, out, S, PL, ST, RH = refs
    else:
        speed, thick, bed, fric, mask, halo, out, S, PL, ST, RH = refs
    levels, own_rows, cols = speed.shape
    lat = lax.axis_index("lat")
    window = ST.shape[1]
    planes = (thick, bed, fric, mask)
    S[:, 0:HALO, :] = jnp.zeros((levels, HALO, cols), F32)
    S[:, HALO + window :, :] = jnp.zeros((levels, HALO, cols), F32)
    PL[:, 0:HALO, :] = jnp.zeros((5, HALO, cols), F32)
    PL[:, HALO + window :, :] = jnp.zeros((5, HALO, cols), F32)

    def place(start, speeds, four):
        rows = pl.ds(pl.multiple_of(HALO + start, 8), speeds.shape[1])
        S[:, rows, :] = speeds
        for n in range(4):
            PL[n, rows, :] = four[n]

    own_four = [thick[...], bed[...], fric[...], mask[...].astype(F32)]
    if masked:
        own_at = HALO
        place(own_at, speed[...], own_four)
        place(0, before[:levels], [before[levels + n] for n in range(4)])
        place(HALO + own_rows, after[:levels], [after[levels + n] for n in range(4)])
    else:
        own_at = lat * HALO
        place(own_at, speed[...], own_four)
        place((1 - lat) * own_rows, halo[:levels], [halo[levels + n] for n in range(4)])
    tiles = range(window // 8)

    def rows_of(t, by=0):
        return slice(HALO + 8 * t + by, HALO + 8 * t + 8 + by)

    PL[4, HALO : HALO + window] = (
        PL[0, HALO : HALO + window] + PL[1, HALO : HALO + window]
    )
    for t in tiles:
        thickness = PL[0, rows_of(t)]
        PL[1, rows_of(t)] = (
            -0.5 * PL[3, rows_of(t)] * thickness * (PL[4, rows_of(t, 1)] - PL[4, rows_of(t, -1)])
        )
    if masked:
        count = lax.axis_size("lat")

        def inside(t):
            row = iota((8, cols), 0) + (8 * t - HALO)
            top = jnp.where(lat == 0, 0, -HALO)
            end = jnp.where(lat == count - 1, own_rows, own_rows + HALO)
            return jnp.logical_and(row >= top, row < end)

    def inverse_of(t):
        thickness = PL[0, rows_of(t)]
        if masked:
            thickness = jnp.where(inside(t), thickness, 1.0)
        return (levels - 1) / thickness

    lanes = iota((8, cols), 1)
    first, last = lanes == 0, lanes == cols - 1

    def sweep(_, carry):
        for t in tiles:
            inverse = inverse_of(t)
            driving = PL[1, rows_of(t)]
            for k in range(levels):
                here = S[k, rows_of(t)]
                north = S[k, rows_of(t, 1)]
                south = S[k, rows_of(t, -1)]
                east = jnp.where(last, 0.0, pltpu.roll(here, cols - 1, 1))
                west = jnp.where(first, 0.0, pltpu.roll(here, 1, 1))
                above = S[min(k + 1, levels - 1), rows_of(t)]
                below = S[max(k - 1, 0), rows_of(t)]
                by_level = (above - below) * inverse
                if k in (0, levels - 1):
                    by_level = 2.0 * by_level
                by_row = north - south
                by_col = east - west
                strain = (
                    0.25 * (by_row * by_row)
                    + 0.0625 * (by_col * by_col + by_level * by_level)
                    + STRAIN_FLOOR
                )
                stiffness = 0.5 * jnp.exp(jnp.log(strain) * (-1.0 / 3.0))
                ST[k, 8 * t : 8 * t + 8] = stiffness
                RH[k, 8 * t : 8 * t + 8] = driving + stiffness * (
                    (north + south) + (east + west)
                )
        scale = [(0.5 * ASPECT) * inverse_of(t) * inverse_of(t) for t in tiles]
        upper, value, vertical, stiff = {}, {}, {}, {}
        for k in range(levels):
            for t in tiles:
                rows = slice(8 * t, 8 * t + 8)
                current = ST[0, rows] if k == 0 else stiff[t]
                diagonal = 4.0 * current
                right = RH[k, rows]
                if k == 0:
                    diagonal = diagonal + PL[2, rows_of(t)]
                else:
                    diagonal = diagonal + vertical[t] * (1.0 - upper[t])
                    right = right + vertical[t] * value[t]
                if k < levels - 1:
                    stiff[t] = ST[k + 1, rows]
                    vertical[t] = scale[t] * (current + stiff[t])
                    diagonal = diagonal + vertical[t]
                invert = 1.0 / diagonal
                value[t] = right * invert
                RH[k, rows] = value[t]
                if k < levels - 1:
                    upper[t] = vertical[t] * invert
                    ST[k, rows] = upper[t]
        for k in range(levels - 1, -1, -1):
            for t in tiles:
                rows = slice(8 * t, 8 * t + 8)
                if k < levels - 1:
                    value[t] = RH[k, rows] + ST[k, rows] * value[t]
                fresh = value[t]
                if masked:
                    fresh = jnp.where(inside(t), fresh, 0.0)
                    value[t] = fresh
                S[k, rows_of(t)] = fresh
        return carry

    lax.fori_loop(0, SWEEPS, sweep, 0)
    for t in tiles:
        total = S[0, rows_of(t)]
        for k in range(1, levels):
            total = total + S[k, rows_of(t)]
        PL[4, rows_of(t)] = PL[0, rows_of(t)] * total * (1.0 / levels)
    for t in tiles:
        fresh = PL[0, rows_of(t)] - 0.25 * (PL[4, rows_of(t, 1)] - PL[4, rows_of(t, -1)])
        PL[1, rows_of(t)] = PL[3, rows_of(t)] * fresh
    out[...] = PL[1, pl.ds(pl.multiple_of(HALO + own_at, 8), own_rows), :].astype(BF16)


def ice_load_of(speed, thick, bed, fric, mask):
    levels, own_rows, cols = speed.shape
    count = lax.axis_size("lat")

    def edge(at):
        return jnp.concatenate(
            [
                speed[:, at : at + HALO],
                thick[None, at : at + HALO],
                bed[None, at : at + HALO],
                fric[None, at : at + HALO],
                mask[None, at : at + HALO].astype(F32),
            ],
            0,
        )

    low, high = edge(0), edge(own_rows - HALO)
    if count == 2:
        sent = jnp.where(lax.axis_index("lat") == 0, high, low)
        halos = [lax.ppermute(sent, "lat", [(0, 1), (1, 0)])]
        window = own_rows + HALO
    else:
        halos = [
            lax.ppermute(high, "lat", [(i, i + 1) for i in range(count - 1)]),
            lax.ppermute(low, "lat", [(i + 1, i) for i in range(count - 1)]),
        ]
        window = own_rows + 2 * HALO
    return pl.pallas_call(
        functools.partial(ice_kernel, masked=count != 2),
        out_shape=jax.ShapeDtypeStruct((own_rows, cols), BF16),
        in_specs=[vmem()] * (5 + len(halos)),
        out_specs=vmem(),
        scratch_shapes=[
            pltpu.VMEM((levels, window + 2 * HALO, cols), F32),
            pltpu.VMEM((5, window + 2 * HALO, cols), F32),
            pltpu.VMEM((levels, window, cols), F32),
            pltpu.VMEM((levels, window, cols), F32),
        ],
        name="ice",
    )(speed, thick, bed, fric, mask, *halos)


def stencil_tables():
    pick_row = np.zeros((32 * COMPS, 24), np.float32)
    pick_col = np.zeros((4, 24, 3 * VEC), np.float32)
    keep = np.zeros((4, 32 * COMPS, 3 * VEC), np.float32)
    for c in range(COMPS):
        for p in range(2):
            for s in range(2):
                for q in range(2):
                    for layer in range(LAYERS):
                        m = ((c * 2 + p) * 2 + s) * PAIR + q * LAYERS + layer
                        pick_row[m, 3 * (4 * p + 2 * q + s) + c] = 1.0
                        for dj in range(3):
                            for c2 in range(COMPS):
                                for q2 in range(2):
                                    for l2 in range(LAYERS):
                                        n = dj * VEC + c2 * PAIR + q2 * LAYERS + l2
                                        p2 = l2 - layer + p
                                        s2 = dj - 1 + s
                                        if p2 in (0, 1) and s2 in (0, 1):
                                            keep[2 * p2 + s2, m, n] = 1.0
    for p2 in range(2):
        for s2 in range(2):
            for dj in range(3):
                for c2 in range(COMPS):
                    for q2 in range(2):
                        for l2 in range(LAYERS):
                            n = dj * VEC + c2 * PAIR + q2 * LAYERS + l2
                            pick_col[2 * p2 + s2, 3 * (4 * p2 + 2 * q2 + s2) + c2, n] = 1.0
    return pick_row, pick_col, keep


def stencil_kernel(matrix, pick_row, pick_col, keep, out, theta):
    exact = functools.partial(
        jnp.dot, precision=lax.Precision.HIGHEST, preferred_element_type=F32
    )
    entries = matrix[...]
    rows = exact(pick_row[...], entries)
    full = jnp.zeros((rows.shape[0], 3 * VEC), F32)
    for n in range(4):
        full = full + keep[n] * exact(rows, pick_col[n])
    high = full.astype(BF16).astype(F32)
    low = full - high
    blank = jnp.zeros((rows.shape[0], PAIR), F32)
    parts = []
    for dj in range(3):
        cut = slice(dj * VEC, (dj + 1) * VEC)
        parts += [high[:, cut], high[:, cut], low[:, cut], blank]
    out[...] = jnp.concatenate(parts, 1).astype(BF16)
    square = iota(entries.shape, 0) == iota(entries.shape, 1)
    trace = jnp.sum(jnp.where(square, entries, 0.0), keepdims=True)
    theta[...] = jnp.broadcast_to(trace * (8.0 * TYPICAL_MODULUS / 24.0), (8, 128))


def stencil_of(matrix):
    tables = [jnp.asarray(t) for t in stencil_tables()]
    return pl.pallas_call(
        stencil_kernel,
        out_shape=(
            jax.ShapeDtypeStruct((32 * COMPS, 3 * (3 * VEC + PAIR)), BF16),
            jax.ShapeDtypeStruct((8, 128), F32),
        ),
        in_specs=[vmem()] * 4,
        out_specs=(vmem(), vmem()),
        name="stencil",
    )(matrix, *tables)


def element_force(vector, stencil, coef):
    parts = []
    for moved in (shift_lanes(vector, -1), vector, shift_lanes(vector, 1)):
        high = moved.astype(BF16).astype(F32)
        low = moved - high
        parts += [high, low, high, low[:PAIR]]
    stacked = jnp.concatenate(parts, 0).astype(BF16)
    force = jnp.dot(stencil, stacked, preferred_element_type=F32)
    sums = []
    for c in range(COMPS):
        total = None
        for n in range(4):
            piece = force[(c * 4 + n) * PAIR : (c * 4 + n + 1) * PAIR] * coef(n)
            total = piece if total is None else total + piece
        sums.append(total)
    return jnp.concatenate(sums, 0)


def swap_rows(x):
    return jnp.concatenate(
        [pltpu.roll(x[c * PAIR : (c + 1) * PAIR], LAYERS, 0) for c in range(COMPS)], 0
    )


def at(base, size, index):
    start = index * size
    if not isinstance(index, int):
        start = pl.multiple_of(start, 8)
    return base.at[pl.ds(start, size)]


def apply_rows(source, coefs, stencil, forces, start, stop, width, store):
    blocks = -(-(stop - start + 2) // width)
    low = min(start - 1, 32 - blocks * width)
    weights = stencil[...]

    def force_block(n, carry):
        base = low + n * width
        for w in range(width):
            pair = base + w
            vector = at(source, VEC, pair)[...]
            coef = at(coefs, 4 * PAIR, pair)
            at(forces, VEC, pair)[...] = element_force(
                vector, weights, lambda n: coef[n * PAIR : (n + 1) * PAIR]
            )
        return carry

    lax.fori_loop(0, blocks, force_block, 0)
    front = iota((VEC, source.shape[1]), 0) % PAIR < LAYERS

    def store_block(n, carry):
        pair = start + n
        before = at(forces, VEC, pair - 1)[...]
        after = at(forces, VEC, pair + 1)[...]
        total = at(forces, VEC, pair)[...] + swap_rows(jnp.where(front, after, before))
        store(pair, total)
        return carry

    lax.fori_loop(0, stop - start, store_block, 0)


def domain_of(pair, cols, group, own_rows, sub):
    row = (pair - 1 - HALO) + group * own_rows + (sub % PAIR) // LAYERS
    shell = (lax.axis_size("group") - 1) * own_rows
    return jnp.where(jnp.logical_and(row >= 0, row < shell), 1.0, 0.0)


def relax_kernel(*refs, pieces):
    E = refs[:pieces]
    stencil, theta = refs[pieces : pieces + 2]
    r_out, c_out, x_out, lw_out, ut_out = refs[pieces + 2 : pieces + 7]
    XP, CR, FO, XS, SH, VI, IW = refs[pieces + 7 :]
    group, lat, rad = (lax.axis_index(n) for n in ("group", "lat", "rad"))
    lat_count = lax.axis_size("lat")
    rows, width = E[0].shape[-2:]
    own_rows = rows - 2 * HALO
    cols = XP.shape[1]
    rad_layers = LAYERS // 2
    planes = COMPS * rad_layers

    def block(lb, rb, plane):
        if pieces == 1:
            return E[0][lb * 2 + rb, plane]
        near, far = [
            jnp.where(rad == rb, E[n][plane], E[n + 1][plane]) for n in (0, 2)
        ]
        return jnp.where(lat == lb, near, far)

    for lb in range(lat_count):
        for rb in range(2):
            for k in range(rad_layers):
                layer = rb * rad_layers + k
                for c in range(COMPS):
                    value = block(lb, rb, c * rad_layers + k)
                    for q in range(2):
                        first = (1 - q) * VEC + c * PAIR + q * LAYERS + layer
                        XS[lb, pl.ds(first, rows, VEC), :] = value
                for ref, plane in ((SH, planes + k), (VI, planes + rad_layers + k)):
                    value = block(lb, rb, plane)
                    for q in range(2):
                        first = (1 - q) * PAIR + q * LAYERS + layer
                        ref[lb, pl.ds(first, rows, PAIR), :] = value
        value = block(lb, 0, planes + 2 * rad_layers)
        for q in range(2):
            for layer in range(LAYERS):
                first = (1 - q) * PAIR + q * LAYERS + layer
                IW[lb, pl.ds(first, rows, PAIR), :] = value

    sub8 = iota((PAIR, cols), 0)
    sub24 = iota((VEC, cols), 0)
    layer8 = sub8 % LAYERS
    shrink = 1.0 / theta[0:1, 0:1]

    def corner_means(nodal):
        both = nodal + pltpu.roll(nodal, LAYERS, 0)
        up = jnp.where(layer8 == LAYERS - 1, 0.0, pltpu.roll(both, PAIR - 1, 0))
        down = jnp.where(layer8 == 0, 0.0, pltpu.roll(both, 1, 0))
        result = []
        for side in (both + up, both + down):
            for step in (1, -1):
                result.append(0.125 * (side + shift_lanes(side, step)))
        return result

    def coef_rows(pair, carry):
        domain = domain_of(pair, cols, group, own_rows, sub8)
        shear, viscosity, vector = [
            jnp.concatenate([at(ref.at[lb], size, pair)[...] for lb in range(lat_count)], 1)
            for ref, size in ((SH, PAIR), (VI, PAIR), (XS, VEC))
        ]
        ratio = shear / viscosity
        damp = 1.0 / (1.0 + ratio)
        modulus = domain * shear * damp
        relaxed = modulus * ratio * damp
        main, relax = corner_means(modulus * shrink), corner_means(relaxed)
        main_ref, relax_ref = at(c_out, 4 * PAIR, pair), at(CR, 4 * PAIR, pair)
        for n in range(4):
            main_ref[n * PAIR : (n + 1) * PAIR] = main[n]
            relax_ref[n * PAIR : (n + 1) * PAIR] = relax[n]
        at(XP, VEC, pair)[...] = vector * domain_of(pair, cols, group, own_rows, sub24)
        return carry

    lax.fori_loop(1, 32, coef_rows, 0)

    def store(pair, total):
        at(r_out, VEC, pair)[...] = -domain_of(pair, cols, group, own_rows, sub24) * total

    apply_rows(XP, CR, stencil, FO, 5, 28, 5, store)
    for t in range(own_rows // 2):
        x_out[t * VEC : (t + 1) * VEC] = XP[(HALO + 1 + 2 * t) * VEC : (HALO + 2 + 2 * t) * VEC]

    blocks = lw_out.shape[2] // 3
    map_rows = blocks // 2
    tile_rows = ut_out.shape[1] // 2
    pair_rows = 32 * PAIR
    row = iota((pair_rows, 1), 0)
    is_top = jnp.where(row % LAYERS == 0, -LOAD_SCALE, 0.0)
    top_scale = is_top * domain_of(row // PAIR, 1, group, own_rows, row)
    for lb in range(lat_count):
        table = IW[lb, 0:pair_rows]
        spots = iota((pair_rows, blocks), 1)
        spread = jnp.zeros((pair_rows, blocks), F32)
        for k in range(4):
            index = table[:, k : k + 1].astype(jnp.int32)
            spot = (index % 2) * map_rows + index // 2
            spread = spread + jnp.where(spots == spot, table[:, 4 + k : 5 + k], 0.0)
        loads = spread * top_scale
        high = loads.astype(BF16).astype(F32)
        middle = (loads - high).astype(BF16).astype(F32)
        low = loads - high - middle
        lw_out[lb] = jnp.concatenate([high, middle, low], 1).astype(BF16)
        own = []
        for t in range(own_rows // 2):
            first = (HALO + 1 + 2 * t) * PAIR
            own.append(table[first : first + PAIR])
        own = jnp.concatenate(own, 0)
        spots = iota((own.shape[0], 2 * tile_rows), 1)
        spread = jnp.zeros((own.shape[0], 2 * tile_rows), F32)
        for k in range(4):
            index = own[:, k : k + 1].astype(jnp.int32)
            near = index // 2 - lat * tile_rows
            spot = (index % 2) * tile_rows + near
            spot = jnp.where(jnp.logical_and(near >= 0, near < tile_rows), spot, -1)
            spread = spread + jnp.where(spots == spot, own[:, 4 + k : 5 + k], 0.0)
        ut_out[lb * own.shape[0] : (lb + 1) * own.shape[0]] = spread * (1.0 / LAYERS)


def krylov_kernel(*refs, loads):
    load_refs = refs[:loads]
    stencil, r_in, coefs, x_own, lw, ut = refs[loads : loads + 6]
    payload, v_out = refs[loads + 6 : loads + 8]
    V, FO = refs[loads + 8 :]
    group, lat = lax.axis_index("group"), lax.axis_index("lat")
    lat_count = lax.axis_size("lat")
    cols = r_in.shape[1]
    width = cols // lat_count
    pairs = x_own.shape[0] // VEC
    own_rows = 2 * pairs
    sub24 = iota((VEC, cols), 0)
    if loads == 2:
        own, other = load_refs[0][...], load_refs[1][...]
        own, other = own.astype(F32), other.astype(F32)
        tiles = [jnp.where(lat == 0, own, other), jnp.where(lat == 0, other, own)]
        field = jnp.concatenate(tiles, 0)
    else:
        field = load_refs[0][...].astype(F32)
    half = field.shape[1] // 2
    blocks = jnp.concatenate([field[:, :half], field[:, half:]], 0)
    blocks = jnp.concatenate([blocks] * 3, 0).astype(BF16)
    count = 32 * PAIR
    for lb in range(lat_count):
        top = jnp.dot(lw[lb], blocks, preferred_element_type=F32)
        FO[0:count, lb * width : (lb + 1) * width] = top

    def start(pair, carry):
        vector = at(r_in, VEC, pair)[...]
        top = at(FO, PAIR, pair)[...]
        vector = jnp.concatenate([vector[: 2 * PAIR], vector[2 * PAIR :] + top], 0)
        at(V.at[0], VEC, pair)[...] = vector
        return carry

    lax.fori_loop(5, 28, start, 0)
    for ref in (V.at[0],):
        ref[0 : 5 * VEC] = jnp.zeros((5 * VEC, cols), F32)
        ref[28 * VEC :] = jnp.zeros((5 * VEC, cols), F32)
    for n in range(ITERS):
        low, high = 6 + n, 27 - n
        if n < ITERS - 1:
            for ref in (V.at[n + 1],):
                ref[(low - 2) * VEC : low * VEC] = jnp.zeros((2 * VEC, cols), F32)
                ref[high * VEC : (high + 2) * VEC] = jnp.zeros((2 * VEC, cols), F32)

        def store(pair, total, n=n):
            domain = domain_of(pair, cols, group, own_rows, sub24)
            fresh = domain * total - at(V.at[n], VEC, pair)[...]
            at(V.at[n + 1], VEC, pair)[...] = fresh

        apply_rows(V.at[n], coefs, stencil, FO, low, high, 5 - n % 2, store)

    def fold(x):
        total = None
        for r in range(x.shape[0] // 8):
            for c in range(x.shape[1] // 128):
                piece = x[8 * r : 8 * r + 8, 128 * c : 128 * c + 128]
                total = piece if total is None else total + piece
        return total

    def products(t, sums):
        pair = HALO + 1 + 2 * t
        values = [at(V.at[n], VEC, pair)[...] for n in range(ITERS + 1)]
        return tuple(
            total + fold(values[k // 2] * values[(k + 1) // 2]) for k, total in enumerate(sums)
        )

    sums = lax.fori_loop(
        0, pairs, products, tuple(jnp.zeros((8, 128), F32) for _ in range(2 * ITERS))
    )
    for k in range(2 * ITERS):
        payload[k : k + 1] = jnp.sum(sums[k], 0, keepdims=True)
    fields = []
    for lb in range(lat_count):
        lanes = slice(lb * width, (lb + 1) * width)
        row = [
            jnp.concatenate(
                [x_own[t * VEC + 2 * PAIR : (t + 1) * VEC, lanes] for t in range(pairs)], 0
            )
        ]
        for n in range(ITERS):
            row.append(
                jnp.concatenate(
                    [
                        V[n, (HALO + 1 + 2 * t) * VEC + 2 * PAIR : (HALO + 2 + 2 * t) * VEC, lanes]
                        for t in range(pairs)
                    ],
                    0,
                )
            )
        fields.append(jnp.concatenate(row, 1))
    fields = jnp.concatenate(fields, 0)
    lift = lax.dot_general(
        ut[...],
        fields,
        (((0,), (0,)), ((), ())),
        precision=lax.Precision.HIGHEST,
        preferred_element_type=F32,
    )
    spots = ut.shape[1]
    for n in range(ITERS + 1):
        payload[2 * ITERS + n * spots : 2 * ITERS + (n + 1) * spots] = lift[
            :, n * width : (n + 1) * width
        ]
    own = pl.ds(pl.multiple_of(lat * width, 128), width)
    for n in range(ITERS):
        for t in range(pairs):
            pair = HALO + 1 + 2 * t
            v_out[n, t * VEC : (t + 1) * VEC] = V[n, pair * VEC : (pair + 1) * VEC, own]
    v_out[ITERS] = x_own[:, own]


def finish_kernel(payload, theta, v, bed, disp_out, bed_out, X):
    rad = lax.axis_index("rad")
    moment = [
        jnp.broadcast_to(jnp.sum(payload[k : k + 1], 1, keepdims=True), (8, 128))
        for k in range(2 * ITERS)
    ]

    def product(left, right, size=False):
        by_degree = {}
        for i, a in enumerate(left):
            for j, b in enumerate(right):
                term = a * b
                if size:
                    term = jnp.abs(term)
                by_degree[i + j] = by_degree[i + j] + term if i + j in by_degree else term
        total = None
        for k, weight in by_degree.items():
            term = weight * (jnp.abs(moment[k]) if size else moment[k])
            total = term if total is None else total + term
        return total

    def shifted(poly):
        result = list(poly) + [jnp.zeros((8, 128), F32)]
        for i, a in enumerate(poly):
            result[i + 1] = result[i + 1] + a
        return result

    one, zero = jnp.ones((8, 128), F32), jnp.zeros((8, 128), F32)
    residual, direction, answer = [one], [one], [zero] * ITERS
    norm = moment[0]
    live = None
    for n in range(ITERS):
        image = shifted(direction)
        step = norm / product(direction, image)
        if live is not None:
            step = jnp.where(live, step, 0.0)
        for i, a in enumerate(direction):
            answer[i] = answer[i] + step * a
        if n == ITERS - 1:
            break
        residual = [
            (residual[i] if i < len(residual) else zero) - step * a for i, a in enumerate(image)
        ]
        fresh = product(residual, residual)
        above = fresh > 1e-7 * product(residual, residual, True)
        live = above if live is None else jnp.logical_and(live, above)
        ratio = jnp.where(live, fresh / norm, 0.0)
        direction = [
            a + (ratio * direction[i] if i < len(direction) else zero)
            for i, a in enumerate(residual)
        ]
        norm = jnp.where(live, fresh, 1.0)
    raw = [a[0:1] for a in answer]
    answer = [a / theta[0:1] for a in raw]
    total = v[ITERS]
    for n in range(ITERS):
        total = total + answer[n] * v[n]
    X[...] = total
    layers = disp_out.shape[1]
    pairs = disp_out.shape[2] // 2
    for c in range(COMPS):
        for k in range(layers):
            for q in range(2):
                lower = X[pl.ds(c * PAIR + q * LAYERS + k, pairs, VEC), :]
                upper = X[pl.ds(c * PAIR + q * LAYERS + layers + k, pairs, VEC), :]
                disp_out[c, k, pl.ds(q, pairs, 2), :] = jnp.where(rad == 0, lower, upper)
    rows, cols = bed.shape
    spots = 2 * rows
    base = 2 * ITERS
    lift = payload[base : base + spots]
    for n in range(ITERS):
        lift = lift + answer[n] * payload[base + (n + 1) * spots : base + (n + 2) * spots]
    for h in range(2):
        lanes = slice(h * cols // 2, (h + 1) * cols // 2)
        bed_out[:, lanes] = bed[:, lanes] + UPLIFT_SCALE * lift[h * rows : (h + 1) * rows]


def per_device(
    displacement_prev,
    shear_modulus,
    viscosity,
    element_matrix,
    regrid_index,
    regrid_weight,
    ice_thickness,
    bed_elevation,
    basal_friction,
    ice_mask,
    speed_guess,
):
    groups, lats = lax.axis_size("group"), lax.axis_size("lat")
    rad_layers, own_rows, width = shear_modulus.shape
    tile_rows, map_cols = ice_thickness.shape
    cols = lats * width
    blocks = 2 * tile_rows * lats
    table = jnp.concatenate(
        [
            regrid_index[:, 0].astype(F32),
            regrid_weight[:, 0],
            jnp.zeros((own_rows, width - 8), F32),
        ],
        1,
    )
    packed = jnp.concatenate(
        [
            displacement_prev.reshape(COMPS * rad_layers, own_rows, width),
            shear_modulus,
            viscosity,
            table[None],
        ],
        0,
    )
    ring = [(i, (i + 1) % groups) for i in range(groups)]
    back = [(i, (i - 1) % groups) for i in range(groups)]
    north = lax.ppermute(packed[:, own_rows - HALO :], "group", ring)
    south = lax.ppermute(packed[:, :HALO], "group", back)
    stencil, theta = stencil_of(element_matrix)
    region = jnp.concatenate([north, packed, south], 1)
    if lats == 2:
        pieces = [
            region,
            lax.ppermute(region, "rad", [(0, 1), (1, 0)]),
            lax.ppermute(region, "lat", [(0, 1), (1, 0)]),
            lax.ppermute(region, ("lat", "rad"), [(i, i ^ 3) for i in range(4)]),
        ]
    else:
        pieces = [lax.all_gather(region, ("lat", "rad"))]
    ice_load = ice_load_of(
        speed_guess, ice_thickness, bed_elevation, basal_friction, ice_mask
    )
    if lats == 2:
        loads = [ice_load, lax.ppermute(ice_load, "lat", [(0, 1), (1, 0)])]
    else:
        loads = [lax.all_gather(ice_load, "lat", axis=0, tiled=True)]
    pairs = own_rows // 2
    r_start, coefs, x_own, lw, ut = pl.pallas_call(
        functools.partial(relax_kernel, pieces=len(pieces)),
        out_shape=(
            jax.ShapeDtypeStruct((33 * VEC, cols), F32),
            jax.ShapeDtypeStruct((33 * 4 * PAIR, cols), F32),
            jax.ShapeDtypeStruct((pairs * VEC, cols), F32),
            jax.ShapeDtypeStruct((lats, 32 * PAIR, 3 * blocks), BF16),
            jax.ShapeDtypeStruct((lats * pairs * PAIR, 2 * tile_rows), F32),
        ),
        in_specs=[vmem()] * (len(pieces) + 2),
        out_specs=(vmem(),) * 5,
        scratch_shapes=[
            pltpu.VMEM((33 * VEC, cols), F32),
            pltpu.VMEM((33 * 4 * PAIR, cols), F32),
            pltpu.VMEM((33 * VEC, cols), F32),
            pltpu.VMEM((lats, 33 * VEC, width), F32),
            pltpu.VMEM((lats, 33 * PAIR, width), F32),
            pltpu.VMEM((lats, 33 * PAIR, width), F32),
            pltpu.VMEM((lats, 33 * PAIR, width), F32),
        ],
        name="relax",
    )(*pieces, stencil, theta)
    spots = 2 * tile_rows
    payload, vectors = pl.pallas_call(
        functools.partial(krylov_kernel, loads=len(loads)),
        out_shape=(
            jax.ShapeDtypeStruct((2 * ITERS + (ITERS + 1) * spots, width), F32),
            jax.ShapeDtypeStruct((ITERS + 1, pairs * VEC, width), F32),
        ),
        in_specs=[vmem()] * (len(loads) + 6),
        out_specs=(vmem(), vmem()),
        scratch_shapes=[
            pltpu.VMEM((ITERS + 1, 33 * VEC, cols), F32),
            pltpu.VMEM((33 * VEC, cols), F32),
        ],
        name="krylov",
    )(*loads, stencil, r_start, coefs, x_own, lw, ut)
    step = 1
    while step < groups:
        payload = payload + lax.ppermute(
            payload, "group", [(i, i ^ step) for i in range(groups)]
        )
        step *= 2
    displacement, bed_new = pl.pallas_call(
        finish_kernel,
        out_shape=(
            jax.ShapeDtypeStruct((COMPS, rad_layers, own_rows, width), F32),
            jax.ShapeDtypeStruct((tile_rows, map_cols), F32),
        ),
        in_specs=[vmem()] * 4,
        out_specs=(vmem(), vmem()),
        scratch_shapes=[pltpu.VMEM((pairs * VEC, width), F32)],
        name="finish",
    )(payload, theta, vectors, bed_elevation)
    return displacement, bed_new


def solution(mesh):
    in_specs = (
        P(None, "rad", "group", "lat"),
        P("rad", "group", "lat"),
        P("rad", "group", "lat"),
        P(),
        P("group", "lat", None),
        P("group", "lat", None),
        P("lat", None),
        P("lat", None),
        P("lat", None),
        P("lat", None),
        P(None, "lat", None),
    )
    out_specs = (P(None, "rad", "group", "lat"), P("lat", None))
    return jax.shard_map(
        per_device, mesh=mesh, in_specs=in_specs, out_specs=out_specs, check_vma=False
    )
```

```python
import functools

import jax
import jax.numpy as jnp
import numpy as np
from jax import lax
from jax.experimental import pallas as pl
from jax.experimental.pallas import tpu as pltpu
from jax.sharding import PartitionSpec as P

SWEEPS = 6
ITERS = 4
HALO = 8
COMPS = 3
LAYERS = 4
PAIR = 2 * LAYERS
VEC = COMPS * PAIR
LOAD_SCALE = 20.0
UPLIFT_SCALE = 0.5
ASPECT = 0.01
STRAIN_FLOOR = 0.01
TYPICAL_MODULUS = 2.2

F32 = jnp.float32
BF16 = jnp.bfloat16


def vmem():
    return pl.BlockSpec(memory_space=pltpu.VMEM)


def keep(*arrays):
    return [pltpu.with_memory_space_constraint(a, pltpu.VMEM) for a in arrays]


def call(body, name, out, inputs, scratch=(), specs=None):
    lats = lax.axis_size("lat")
    return pl.pallas_call(
        body,
        out_shape=out,
        in_specs=specs or [vmem()] * len(inputs),
        out_specs=jax.tree.map(lambda _: vmem(), out),
        scratch_shapes=list(scratch),
        compiler_params=pltpu.CompilerParams(vmem_limit_bytes=(8 if lats == 2 else 40) << 20),
        name=name,
    )(*inputs)


def iota(shape, dim):
    return lax.broadcasted_iota(jnp.int32, shape, dim)


def shift_lanes(x, step):
    zero = jnp.zeros((x.shape[0], 1), x.dtype)
    if step == 1:
        return jnp.concatenate([x[:, 1:], zero], 1)
    return jnp.concatenate([zero, x[:, :-1]], 1)


def ice_kernel(*refs, masked):
    if masked:
        speed, thick, bed, fric, mask, before, after, out, S, PL, ST, RH = refs
    else:
        speed, thick, bed, fric, mask, halo, out, S, PL, ST, RH = refs
    levels, own_rows, cols = speed.shape
    lat = lax.axis_index("lat")
    window = ST.shape[1]
    planes = (thick, bed, fric, mask)
    S[:, 0:HALO, :] = jnp.zeros((levels, HALO, cols), F32)
    S[:, HALO + window :, :] = jnp.zeros((levels, HALO, cols), F32)
    PL[:, 0:HALO, :] = jnp.zeros((5, HALO, cols), F32)
    PL[:, HALO + window :, :] = jnp.zeros((5, HALO, cols), F32)

    def place(start, speeds, four):
        rows = pl.ds(pl.multiple_of(HALO + start, 8), speeds.shape[1])
        S[:, rows, :] = speeds
        for n in range(4):
            PL[n, rows, :] = four[n]

    own_four = [thick[...], bed[...], fric[...], mask[...].astype(F32)]
    if masked:
        own_at = HALO
        place(own_at, speed[...], own_four)
        place(0, before[:levels], [before[levels + n] for n in range(4)])
        place(HALO + own_rows, after[:levels], [after[levels + n] for n in range(4)])
    else:
        own_at = lat * HALO
        place(own_at, speed[...], own_four)
        place((1 - lat) * own_rows, halo[:levels], [halo[levels + n] for n in range(4)])
    tiles = range(window // 8)

    def rows_of(t):
        return slice(HALO + 8 * t, HALO + 8 * t + 8)

    sub = iota((8, cols), 0)
    top_row, bottom_row = sub == 0, sub == 7

    def north_of(ref, t, here):
        joined = jnp.where(top_row, ref[rows_of(t + 1)], here)
        return pltpu.roll(joined, 7, 0)

    def south_of(ref, t, here):
        joined = jnp.where(bottom_row, ref[rows_of(t - 1)], here)
        return pltpu.roll(joined, 1, 0)

    factor = 0.5 * 0.25 ** (-1.0 / 3.0)
    PL[4, HALO : HALO + window] = (
        PL[0, HALO : HALO + window] + PL[1, HALO : HALO + window]
    )
    for t in tiles:
        here = PL[4, rows_of(t)]
        PL[1, rows_of(t)] = (
            (-0.5 / factor)
            * PL[3, rows_of(t)]
            * PL[0, rows_of(t)]
            * (north_of(PL.at[4], t, here) - south_of(PL.at[4], t, here))
        )
        PL[2, rows_of(t)] = PL[2, rows_of(t)] * (1.0 / factor)
    if masked:
        count = lax.axis_size("lat")

        def inside(t):
            row = iota((8, cols), 0) + (8 * t - HALO)
            top = jnp.where(lat == 0, 0, -HALO)
            end = jnp.where(lat == count - 1, own_rows, own_rows + HALO)
            return jnp.logical_and(row >= top, row < end)

    def inverse_of(t):
        thickness = PL[0, rows_of(t)]
        if masked:
            thickness = jnp.where(inside(t), thickness, 1.0)
        return (levels - 1) / thickness

    def sweep(_, carry):
        for t in tiles:
            inverse = 0.5 * inverse_of(t)
            driving = PL[1, rows_of(t)]
            for k in range(levels):
                here = S[k, rows_of(t)]
                north, south = north_of(S.at[k], t, here), south_of(S.at[k], t, here)
                east, west = shift_lanes(here, 1), shift_lanes(here, -1)
                above = S[min(k + 1, levels - 1), rows_of(t)]
                below = S[max(k - 1, 0), rows_of(t)]
                by_level = (above - below) * inverse
                if k in (0, levels - 1):
                    by_level = 2.0 * by_level
                by_row = north - south
                by_col = east - west
                strain = (by_row * by_row + 4.0 * STRAIN_FLOOR) + (
                    0.25 * (by_col * by_col) + by_level * by_level
                )
                stiffness = jnp.exp2(jnp.log2(strain) * (-1.0 / 3.0))
                ST[k, 8 * t : 8 * t + 8] = stiffness
                RH[k, 8 * t : 8 * t + 8] = driving + stiffness * (
                    (north + south) + (east + west)
                )
        scale = [(0.5 * ASPECT) * inverse_of(t) * inverse_of(t) for t in tiles]
        upper, value, vertical, stiff, rest = {}, {}, {}, {}, {}
        for k in range(levels):
            for t in tiles:
                rows = slice(8 * t, 8 * t + 8)
                current = ST[0, rows] if k == 0 else stiff[t]
                partial = 4.0 * current
                right = RH[k, rows]
                if k == 0:
                    partial = partial + PL[2, rows_of(t)]
                else:
                    partial = partial + vertical[t] * rest[t]
                    right = right + vertical[t] * value[t]
                diagonal = partial
                if k < levels - 1:
                    stiff[t] = ST[k + 1, rows]
                    vertical[t] = scale[t] * (current + stiff[t])
                    diagonal = partial + vertical[t]
                invert = 1.0 / diagonal
                value[t] = right * invert
                RH[k, rows] = value[t]
                if k < levels - 1:
                    rest[t] = partial * invert
                    ST[k, rows] = vertical[t] * invert
        for k in range(levels - 1, -1, -1):
            for t in tiles:
                rows = slice(8 * t, 8 * t + 8)
                if k < levels - 1:
                    value[t] = RH[k, rows] + ST[k, rows] * value[t]
                fresh = value[t]
                if masked:
                    fresh = jnp.where(inside(t), fresh, 0.0)
                    value[t] = fresh
                S[k, rows_of(t)] = fresh
        return carry

    lax.fori_loop(0, SWEEPS, sweep, 0)
    for t in tiles:
        total = S[0, rows_of(t)]
        for k in range(1, levels):
            total = total + S[k, rows_of(t)]
        PL[4, rows_of(t)] = PL[0, rows_of(t)] * total * (1.0 / levels)
    for t in tiles:
        here = PL[4, rows_of(t)]
        change = north_of(PL.at[4], t, here) - south_of(PL.at[4], t, here)
        fresh = PL[0, rows_of(t)] - 0.25 * change
        PL[1, rows_of(t)] = PL[3, rows_of(t)] * fresh
    out[...] = PL[1, pl.ds(pl.multiple_of(HALO + own_at, 8), own_rows), :].astype(BF16)


def edge_kernel(speed, thick, bed, fric, mask, *rest, masked):
    outs, sems = rest[:-1], rest[-1]
    levels, own_rows, cols = speed.shape
    top = own_rows - HALO
    if masked:
        starts = [0, top]
    else:
        starts = [jnp.where(lax.axis_index("lat") == 0, top, 0)]
    copies = []
    for n, (start, out) in enumerate(zip(starts, outs)):
        rows = pl.ds(start if masked else pl.multiple_of(start, 8), HALO)
        copies.append(
            pltpu.make_async_copy(speed.at[:, rows, :], out.at[0:levels], sems.at[4 * n])
        )
        for m, plane in enumerate((thick, bed, fric)):
            copies.append(
                pltpu.make_async_copy(
                    plane.at[rows, :], out.at[levels + m], sems.at[4 * n + 1 + m]
                )
            )
    for copy in copies:
        copy.start()
    for start, out in zip(starts, outs):
        rows = pl.ds(start if masked else pl.multiple_of(start, 8), HALO)
        out[levels + 3] = mask[rows, :].astype(F32)
    for copy in copies:
        copy.wait()


def ice_edges(speed, thick, bed, fric, mask):
    levels, _, cols = speed.shape
    masked = lax.axis_size("lat") != 2
    count = 2 if masked else 1
    return call(
        functools.partial(edge_kernel, masked=masked),
        "edge",
        (pltpu.VMEM((levels + 4, HALO, cols), F32),) * count,
        (speed, thick, bed, fric, mask),
        [pltpu.SemaphoreType.DMA((4 * count,))],
        [pl.BlockSpec(memory_space=pl.ANY)] * 4 + [vmem()],
    )


def ice_load_of(speed, thick, bed, fric, mask, halos):
    levels, own_rows, cols = speed.shape
    window = own_rows + HALO * (1 if len(halos) == 1 else 2)
    return call(
        functools.partial(ice_kernel, masked=len(halos) != 1),
        "ice",
        pltpu.VMEM((own_rows, cols), BF16),
        (speed, thick, bed, fric, mask, *keep(*halos)),
        [
            pltpu.VMEM((levels, window + 2 * HALO, cols), F32),
            pltpu.VMEM((5, window + 2 * HALO, cols), F32),
            pltpu.VMEM((levels, window, cols), F32),
            pltpu.VMEM((levels, window, cols), F32),
        ],
    )


def stencil_tables():
    pick_row = np.zeros((32 * COMPS, 24), np.float32)
    pick_col = np.zeros((4, 24, 3 * VEC), np.float32)
    keep = np.zeros((4, 32 * COMPS, 3 * VEC), np.float32)
    for c in range(COMPS):
        for p in range(2):
            for s in range(2):
                for q in range(2):
                    for layer in range(LAYERS):
                        m = ((c * 2 + p) * 2 + s) * PAIR + q * LAYERS + layer
                        pick_row[m, 3 * (4 * p + 2 * q + s) + c] = 1.0
                        for dj in range(3):
                            for c2 in range(COMPS):
                                for q2 in range(2):
                                    for l2 in range(LAYERS):
                                        n = dj * VEC + c2 * PAIR + q2 * LAYERS + l2
                                        p2 = l2 - layer + p
                                        s2 = dj - 1 + s
                                        if p2 in (0, 1) and s2 in (0, 1):
                                            keep[2 * p2 + s2, m, n] = 1.0
    for p2 in range(2):
        for s2 in range(2):
            for dj in range(3):
                for c2 in range(COMPS):
                    for q2 in range(2):
                        for l2 in range(LAYERS):
                            n = dj * VEC + c2 * PAIR + q2 * LAYERS + l2
                            pick_col[2 * p2 + s2, 3 * (4 * p2 + 2 * q2 + s2) + c2, n] = 1.0
    return pick_row, pick_col, keep


def stencil_kernel(matrix, pick_row, pick_col, keep, out, theta):
    exact = functools.partial(
        jnp.dot, precision=lax.Precision.HIGHEST, preferred_element_type=F32
    )
    entries = matrix[...]
    rows = exact(pick_row[...], entries)
    full = jnp.zeros((rows.shape[0], 3 * VEC), F32)
    for n in range(4):
        full = full + keep[n] * exact(rows, pick_col[n])
    high = full.astype(BF16).astype(F32)
    low = full - high
    blank = jnp.zeros((rows.shape[0], PAIR), F32)
    parts = []
    for dj in range(3):
        cut = slice(dj * VEC, (dj + 1) * VEC)
        parts += [high[:, cut], high[:, cut], low[:, cut], blank]
    out[...] = jnp.concatenate(parts, 1).astype(BF16)
    square = iota(entries.shape, 0) == iota(entries.shape, 1)
    trace = jnp.sum(jnp.where(square, entries, 0.0), keepdims=True)
    theta[...] = jnp.broadcast_to(trace * (8.0 * TYPICAL_MODULUS / 24.0), (8, 128))


def stencil_of(matrix):
    tables = [jnp.asarray(t) for t in stencil_tables()]
    return call(
        stencil_kernel,
        "stencil",
        (
            pltpu.VMEM((32 * COMPS, 3 * (3 * VEC + PAIR)), BF16),
            pltpu.VMEM((8, 128), F32),
        ),
        (matrix, *tables),
    )


def pack_kernel(disp, shear, visc, index, weight, low, high, TS, *, map_rows):
    layers = shear.shape[0]
    count = COMPS * layers
    spot = index[...]
    TS[0:4, 0 : 2 * HALO] = ((spot % 2) * map_rows + spot // 2).astype(F32)
    TS[4:8, 0 : 2 * HALO] = weight[...]
    table = jnp.transpose(TS[...])
    for n, out in enumerate((low, high)):
        rows = slice(n * HALO, (n + 1) * HALO)
        for c in range(COMPS):
            for k in range(layers):
                out[c * layers + k] = disp[c, k, rows]
        for k in range(layers):
            out[count + k] = shear[k, rows]
            out[count + layers + k] = visc[k, rows]
        out[count + 2 * layers, :, 0:8] = table[rows]


def region_kernel(north, low, high, south, out):
    for n, piece in enumerate((north, low, high, south)):
        out[:, n * HALO : (n + 1) * HALO] = piece[...]


def at(base, size, index):
    return base.at[pl.ds(index * size, size)]


def element_force(vector, stencil, coef):
    high = vector.astype(BF16).astype(F32)
    split = jnp.concatenate([high, vector - high], 0).astype(BF16)
    parts = []
    for moved in (shift_lanes(split, -1), split, shift_lanes(split, 1)):
        parts += [moved, moved[: VEC + PAIR]]
    force = jnp.dot(stencil, jnp.concatenate(parts, 0), preferred_element_type=F32)
    sums = []
    for c in range(COMPS):
        total = None
        for n in range(4):
            first = (c * 4 + n) * PAIR
            piece = force[first : first + PAIR] * coef[n * PAIR : (n + 1) * PAIR]
            total = piece if total is None else total + piece
        sums.append(total)
    return sums


def apply_rows(source, coefs, stencil, start, stop, store):
    weights = stencil[...]
    front = iota((PAIR, source.shape[1]), 0) < LAYERS
    forces = {}
    for pair in range(start - 1, stop + 1):
        forces[pair] = element_force(
            at(source, VEC, pair)[...], weights, at(coefs, 4 * PAIR, pair)[...]
        )
        done = pair - 1
        if done >= start:
            sums = []
            for c in range(COMPS):
                swapped = jnp.where(front, forces[pair][c], forces[done - 1][c])
                sums.append(forces[done][c] + pltpu.roll(swapped, LAYERS, 0))
            store(done, sums)
            del forces[done - 1]


def domain_of(own_rows, cols):
    shell = (lax.axis_size("group") - 1) * own_rows
    base = iota((PAIR, 128), 0) // LAYERS + lax.axis_index("group") * own_rows

    def mask(pair):
        offset = pair - 1 - HALO
        live = jnp.logical_and(base >= -offset, base < shell - offset)
        one = jnp.where(live, 1.0, 0.0)
        return jnp.concatenate([one] * (cols // 128), 1)

    return mask


def relax_kernel(*refs, pieces):
    E = refs[:pieces]
    stencil, theta = refs[pieces : pieces + 2]
    r_out, c_out, x_out, lw_out, ut_out = refs[pieces + 2 : pieces + 7]
    XP, CR, XS, SH, VI = refs[pieces + 7 :]
    group, lat, rad = (lax.axis_index(n) for n in ("group", "lat", "rad"))
    lat_count = lax.axis_size("lat")
    rows, width = E[0].shape[-2:]
    own_rows = rows - 2 * HALO
    cols = XP.shape[1]
    rad_layers = LAYERS // 2
    planes = COMPS * rad_layers

    def block(lb, rb, plane):
        if pieces == 1:
            return E[0][lb * 2 + rb, plane]
        near, far = [
            jnp.where(rad == rb, E[n][plane], E[n + 1][plane]) for n in (0, 2)
        ]
        return jnp.where(lat == lb, near, far)

    for lb in range(lat_count):
        for rb in range(2):
            for k in range(rad_layers):
                layer = rb * rad_layers + k
                for c in range(COMPS):
                    value = block(lb, rb, c * rad_layers + k)
                    for q in range(2):
                        first = (1 - q) * VEC + c * PAIR + q * LAYERS + layer
                        XS[lb, pl.ds(first, rows, VEC), :] = value
                for ref, plane in ((SH, planes + k), (VI, planes + rad_layers + k)):
                    value = block(lb, rb, plane)
                    for q in range(2):
                        first = (1 - q) * PAIR + q * LAYERS + layer
                        ref[lb, pl.ds(first, rows, PAIR), :] = value

    mask = domain_of(own_rows, cols)
    layer8 = iota((PAIR, cols), 0) % LAYERS
    top_layer, last_layer = layer8 == 0, layer8 == LAYERS - 1
    shrink = 1.0 / theta[0:1, 0:1]
    eighth = 0.125 * shrink

    def corner_means(nodal, scale):
        both = nodal + pltpu.roll(nodal, LAYERS, 0)
        up = jnp.where(last_layer, 0.0, pltpu.roll(both, PAIR - 1, 0))
        down = jnp.where(top_layer, 0.0, pltpu.roll(both, 1, 0))
        result = []
        for side in (both + up, both + down):
            side = scale * side
            for step in (1, -1):
                result.append(side + shift_lanes(side, step))
        return jnp.concatenate(result, 0)

    for pair in range(4, 29):
        domain = mask(pair)
        shear, viscosity, vector = [
            jnp.concatenate([at(ref.at[lb], size, pair)[...] for lb in range(lat_count)], 1)
            for ref, size in ((SH, PAIR), (VI, PAIR), (XS, VEC))
        ]
        ratio = shear / viscosity
        damp = 1.0 / (1.0 + ratio)
        modulus = domain * shear * damp
        relaxed = modulus * ratio * damp
        at(c_out, 4 * PAIR, pair)[...] = corner_means(modulus, eighth)
        at(CR, 4 * PAIR, pair)[...] = corner_means(relaxed, 0.125)
        at(XP, VEC, pair)[...] = vector * jnp.concatenate([domain] * COMPS, 0)

    def store(pair, sums):
        domain = mask(pair)
        at(r_out, VEC, pair)[...] = jnp.concatenate([-domain * x for x in sums], 0)

    apply_rows(XP, CR, stencil, 5, 28, store)
    for t in range(own_rows // 2):
        x_out[t * VEC : (t + 1) * VEC] = at(XP, VEC, HALO + 1 + 2 * t)[...]

    blocks = lw_out.shape[2] // 3
    map_rows = blocks // 2
    tile_rows = map_rows // lat_count
    row = iota((rows, 1), 0) - HALO + group * own_rows
    shell = (lax.axis_size("group") - 1) * own_rows
    scale = jnp.where(jnp.logical_and(row >= 0, row < shell), -LOAD_SCALE, 0.0)
    own = slice(HALO, HALO + own_rows)
    for lb in range(lat_count):
        table = block(lb, 0, planes + 2 * rad_layers)
        spots = iota((rows, blocks), 1).astype(F32)
        own_spots = iota((own_rows, 128), 1).astype(F32)
        loads = jnp.zeros((rows, blocks), F32)
        lift = jnp.zeros((own_rows, 128), F32)
        for k in range(4):
            index, weight = table[:, k : k + 1], table[:, 4 + k : 5 + k]
            loads = loads + jnp.where(spots == index, weight, 0.0)
            right = index[own] >= map_rows
            near = index[own] - jnp.where(right, map_rows, 0) - (lat * tile_rows).astype(F32)
            here = jnp.logical_and(near >= 0, near < tile_rows)
            spot = jnp.where(here, near + jnp.where(right, tile_rows, 0), -1.0)
            lift = lift + jnp.where(own_spots == spot, weight[own], 0.0)
        loads = loads * scale
        high = loads.astype(BF16).astype(F32)
        middle = (loads - high).astype(BF16).astype(F32)
        low = loads - high - middle
        lw_out[lb] = jnp.concatenate([high, middle, low], 1).astype(BF16)
        lift = lift * (1.0 / LAYERS)
        for layer in range(LAYERS):
            first = lb * own_rows * LAYERS + layer
            ut_out[pl.ds(first, own_rows, LAYERS), :] = lift


def krylov_kernel(*refs, loads):
    load_refs = refs[:loads]
    stencil, r_in, coefs, x_own, lw, ut = refs[loads : loads + 6]
    payload, v_out = refs[loads + 6 : loads + 8]
    V, TOP = refs[loads + 8 :]
    lat = lax.axis_index("lat")
    lat_count = lax.axis_size("lat")
    cols = r_in.shape[1]
    width = cols // lat_count
    pairs = x_own.shape[0] // VEC
    own_rows = 2 * pairs
    if loads == 2:
        own, other = load_refs[0][...], load_refs[1][...]
        own, other = own.astype(F32), other.astype(F32)
        tiles = [jnp.where(lat == 0, own, other), jnp.where(lat == 0, other, own)]
        field = jnp.concatenate(tiles, 0)
    else:
        field = load_refs[0][...].astype(F32)
    half = field.shape[1] // 2
    blocks = jnp.concatenate([field[:, :half], field[:, half:]], 0)
    blocks = jnp.concatenate([blocks] * 3, 0).astype(BF16)
    for lb in range(lat_count):
        TOP[lb] = jnp.zeros(TOP.shape[1:], F32)
        top = jnp.dot(lw[lb], blocks, preferred_element_type=F32)
        for q in range(2):
            TOP[lb, pl.ds((1 - q) * PAIR + q * LAYERS, top.shape[0], PAIR), :] = top
    for pair in range(5, 28):
        vector = at(r_in, VEC, pair)[...]
        top = [at(TOP.at[lb], PAIR, pair)[...] for lb in range(lat_count)]
        upright = vector[2 * PAIR :] + jnp.concatenate(top, 1)
        at(V.at[0], VEC, pair)[...] = jnp.concatenate([vector[: 2 * PAIR], upright], 0)
    mask = domain_of(own_rows, cols)
    for n in range(ITERS):

        def store(pair, sums, n=n):
            domain = mask(pair)
            fresh = jnp.concatenate([domain * x for x in sums], 0)
            at(V.at[n + 1], VEC, pair)[...] = fresh - at(V.at[n], VEC, pair)[...]

        apply_rows(V.at[n], coefs, stencil, 6 + n, 27 - n, store)

    own_pairs = [HALO + 1 + 2 * t for t in range(pairs)]
    sums = [None] * (2 * ITERS)
    for pair in own_pairs:
        values = [at(V.at[n], VEC, pair)[...] for n in range(ITERS + 1)]
        for k in range(2 * ITERS):
            product = values[k // 2] * values[(k + 1) // 2]
            for r in range(COMPS):
                for c in range(cols // 128):
                    piece = product[PAIR * r : PAIR * r + PAIR, 128 * c : 128 * c + 128]
                    sums[k] = piece if sums[k] is None else sums[k] + piece
    for k in range(2 * ITERS):
        payload[k : k + 1] = jnp.sum(sums[k], 0, keepdims=True)
    fields = []
    upright = slice(2 * PAIR, VEC)
    for lb in range(lat_count):
        lanes = slice(lb * width, (lb + 1) * width)
        row = [[x_own[t * VEC + 2 * PAIR : (t + 1) * VEC, lanes] for t in range(pairs)]]
        for n in range(ITERS):
            row.append([at(V.at[n], VEC, pair)[upright, lanes] for pair in own_pairs])
        fields.append(jnp.concatenate([jnp.concatenate(x, 0) for x in row], 1))
    fields = jnp.concatenate(fields, 0)
    spots = (payload.shape[0] - 2 * ITERS) // (ITERS + 1)
    lift = lax.dot_general(
        ut[...],
        fields,
        (((0,), (0,)), ((), ())),
        precision=lax.Precision.HIGHEST,
        preferred_element_type=F32,
    )
    for n in range(ITERS + 1):
        payload[2 * ITERS + n * spots : 2 * ITERS + (n + 1) * spots] = lift[
            :spots, n * width : (n + 1) * width
        ]
    own = pl.ds(pl.multiple_of(lat * width, 128), width)
    for n in range(ITERS):
        for t, pair in enumerate(own_pairs):
            v_out[n, t * VEC : (t + 1) * VEC] = V[n, pair * VEC : (pair + 1) * VEC, own]
    v_out[ITERS] = x_own[:, own]


def finish_kernel(payload, theta, v, bed, disp_out, bed_out, X):
    rad = lax.axis_index("rad")
    moment = [
        jnp.broadcast_to(jnp.sum(payload[k : k + 1], 1, keepdims=True), (8, 128))
        for k in range(2 * ITERS)
    ]

    def product(left, right, size=False):
        by_degree = {}
        for i, a in enumerate(left):
            for j, b in enumerate(right):
                term = a * b
                if size:
                    term = jnp.abs(term)
                by_degree[i + j] = by_degree[i + j] + term if i + j in by_degree else term
        total = None
        for k, weight in by_degree.items():
            term = weight * (jnp.abs(moment[k]) if size else moment[k])
            total = term if total is None else total + term
        return total

    def shifted(poly):
        result = list(poly) + [jnp.zeros((8, 128), F32)]
        for i, a in enumerate(poly):
            result[i + 1] = result[i + 1] + a
        return result

    one, zero = jnp.ones((8, 128), F32), jnp.zeros((8, 128), F32)
    residual, direction, answer = [one], [one], [zero] * ITERS
    norm = moment[0]
    live = None
    for n in range(ITERS):
        image = shifted(direction)
        step = norm / product(direction, image)
        if live is not None:
            step = jnp.where(live, step, 0.0)
        for i, a in enumerate(direction):
            answer[i] = answer[i] + step * a
        if n == ITERS - 1:
            break
        residual = [
            (residual[i] if i < len(residual) else zero) - step * a for i, a in enumerate(image)
        ]
        fresh = product(residual, residual)
        above = fresh > 1e-7 * product(residual, residual, True)
        live = above if live is None else jnp.logical_and(live, above)
        ratio = jnp.where(live, fresh / norm, 0.0)
        direction = [
            a + (ratio * direction[i] if i < len(direction) else zero)
            for i, a in enumerate(residual)
        ]
        norm = jnp.where(live, fresh, 1.0)
    raw = [a[0:1] for a in answer]
    answer = [a / theta[0:1] for a in raw]
    total = v[ITERS]
    for n in range(ITERS):
        total = total + answer[n] * v[n]
    X[...] = total
    layers = disp_out.shape[1]
    pairs = disp_out.shape[2] // 2
    for c in range(COMPS):
        for k in range(layers):
            for q in range(2):
                lower = X[pl.ds(c * PAIR + q * LAYERS + k, pairs, VEC), :]
                upper = X[pl.ds(c * PAIR + q * LAYERS + layers + k, pairs, VEC), :]
                disp_out[c, k, pl.ds(q, pairs, 2), :] = jnp.where(rad == 0, lower, upper)
    rows, cols = bed.shape
    spots = 2 * rows
    base = 2 * ITERS
    lift = payload[base : base + spots]
    for n in range(ITERS):
        lift = lift + answer[n] * payload[base + (n + 1) * spots : base + (n + 2) * spots]
    for h in range(2):
        lanes = slice(h * cols // 2, (h + 1) * cols // 2)
        bed_out[:, lanes] = bed[:, lanes] + UPLIFT_SCALE * lift[h * rows : (h + 1) * rows]


def per_device(
    displacement_prev,
    shear_modulus,
    viscosity,
    element_matrix,
    regrid_index,
    regrid_weight,
    ice_thickness,
    bed_elevation,
    basal_friction,
    ice_mask,
    speed_guess,
):
    groups, lats = lax.axis_size("group"), lax.axis_size("lat")
    rad_layers, own_rows, width = shear_modulus.shape
    tile_rows, map_cols = ice_thickness.shape
    cols = lats * width
    blocks = 2 * tile_rows * lats
    planes = COMPS * rad_layers + 2 * rad_layers + 1
    ice_args = (speed_guess, ice_thickness, bed_elevation, basal_friction, ice_mask)

    edges = ice_edges(*ice_args)
    if lats == 2:
        halos = [lax.ppermute(edges[0], "lat", [(0, 1), (1, 0)])]
    else:
        halos = [
            lax.ppermute(edges[1], "lat", [(i, i + 1) for i in range(lats - 1)]),
            lax.ppermute(edges[0], "lat", [(i + 1, i) for i in range(lats - 1)]),
        ]
    low, high = call(
        functools.partial(pack_kernel, map_rows=tile_rows * lats),
        "pack",
        (pltpu.VMEM((planes, HALO, width), F32),) * 2,
        (
            displacement_prev,
            shear_modulus,
            viscosity,
            regrid_index[:, 0].T,
            regrid_weight[:, 0].T,
        ),
        [pltpu.VMEM((8, 128), F32)],
    )
    north = lax.ppermute(high, "group", [(i, (i + 1) % groups) for i in range(groups)])
    south = lax.ppermute(low, "group", [(i, (i - 1) % groups) for i in range(groups)])
    stencil, theta = stencil_of(element_matrix)
    region = call(
        region_kernel,
        "region",
        pltpu.VMEM((planes, 2 * own_rows, width), F32),
        keep(north, low, high, south),
    )
    if lats == 2:
        pieces = [region, lax.ppermute(region, "rad", [(0, 1), (1, 0)])]
        region, halos = lax.optimization_barrier((region, halos))
        pieces.append(lax.ppermute(region, "lat", [(0, 1), (1, 0)]))
        pieces.append(lax.ppermute(pieces[2], "rad", [(0, 1), (1, 0)]))
    else:
        pieces = [lax.all_gather(region, ("lat", "rad"))]
    ice_load = ice_load_of(*ice_args, halos)
    if lats == 2:
        loads = [ice_load, lax.ppermute(ice_load, "lat", [(0, 1), (1, 0)])]
    else:
        loads = [lax.all_gather(ice_load, "lat", axis=0, tiled=True)]
    pairs = own_rows // 2
    r_start, coefs, x_own, lw, ut = call(
        functools.partial(relax_kernel, pieces=len(pieces)),
        "relax",
        (
            pltpu.VMEM((33 * VEC, cols), F32),
            pltpu.VMEM((33 * 4 * PAIR, cols), F32),
            pltpu.VMEM((pairs * VEC, cols), F32),
            pltpu.VMEM((lats, 2 * own_rows, 3 * blocks), BF16),
            pltpu.VMEM((lats * own_rows * LAYERS, 128), F32),
        ),
        keep(*pieces, stencil, theta),
        [
            pltpu.VMEM((33 * VEC, cols), F32),
            pltpu.VMEM((33 * 4 * PAIR, cols), F32),
            pltpu.VMEM((lats, 33 * VEC, width), F32),
            pltpu.VMEM((lats, 33 * PAIR, width), F32),
            pltpu.VMEM((lats, 33 * PAIR, width), F32),
        ],
    )
    spots = 2 * tile_rows
    payload, vectors = call(
        functools.partial(krylov_kernel, loads=len(loads)),
        "krylov",
        (
            pltpu.VMEM((2 * ITERS + (ITERS + 1) * spots, width), F32),
            pltpu.VMEM((ITERS + 1, pairs * VEC, width), F32),
        ),
        keep(*loads, stencil, r_start, coefs, x_own, lw, ut),
        [
            pltpu.VMEM((ITERS + 1, 33 * VEC, cols), F32),
            pltpu.VMEM((lats, 33 * PAIR, width), F32),
        ],
    )
    step = 1
    while step < groups:
        payload = payload + lax.ppermute(
            payload, "group", [(i, i ^ step) for i in range(groups)]
        )
        step *= 2
    return call(
        finish_kernel,
        "finish",
        (
            jax.ShapeDtypeStruct((COMPS, rad_layers, own_rows, width), F32),
            jax.ShapeDtypeStruct((tile_rows, map_cols), F32),
        ),
        (*keep(payload, theta, vectors), bed_elevation),
        [pltpu.VMEM((pairs * VEC, width), F32)],
    )


def solution(mesh):
    in_specs = (
        P(None, "rad", "group", "lat"),
        P("rad", "group", "lat"),
        P("rad", "group", "lat"),
        P(),
        P("group", "lat", None),
        P("group", "lat", None),
        P("lat", None),
        P("lat", None),
        P("lat", None),
        P("lat", None),
        P(None, "lat", None),
    )
    out_specs = (P(None, "rad", "group", "lat"), P("lat", None))
    return jax.shard_map(
        per_device, mesh=mesh, in_specs=in_specs, out_specs=out_specs, check_vma=False
    )
```

```python
import functools

import jax
import jax.numpy as jnp
import numpy as np
from jax import lax
from jax.experimental import pallas as pl
from jax.experimental.pallas import tpu as pltpu
from jax.sharding import PartitionSpec as P

SWEEPS = 6
ITERS = 4
HALO = 8
COMPS = 3
LAYERS = 4
PAIR = 2 * LAYERS
VEC = COMPS * PAIR
LOAD_SCALE = 20.0
UPLIFT_SCALE = 0.5
ASPECT = 0.01
STRAIN_FLOOR = 0.01
TYPICAL_MODULUS = 2.2

F32 = jnp.float32
BF16 = jnp.bfloat16


def vmem():
    return pl.BlockSpec(memory_space=pltpu.VMEM)


def keep(*arrays):
    return [pltpu.with_memory_space_constraint(a, pltpu.VMEM) for a in arrays]


def leave(*arrays):
    return [pltpu.with_memory_space_constraint(a, pltpu.HBM) for a in arrays]


def call(body, name, out, inputs, scratch=(), specs=None):
    lats = lax.axis_size("lat")
    return pl.pallas_call(
        body,
        out_shape=out,
        in_specs=specs or [vmem()] * len(inputs),
        out_specs=jax.tree.map(lambda _: vmem(), out),
        scratch_shapes=list(scratch),
        compiler_params=pltpu.CompilerParams(vmem_limit_bytes=(8 if lats == 2 else 40) << 20),
        name=name,
    )(*inputs)


def iota(shape, dim):
    return lax.broadcasted_iota(jnp.int32, shape, dim)


def shift_lanes(x, step):
    zero = jnp.zeros((x.shape[0], 1), x.dtype)
    if step == 1:
        return jnp.concatenate([x[:, 1:], zero], 1)
    return jnp.concatenate([zero, x[:, :-1]], 1)


def ice_kernel(*refs, masked):
    if masked:
        speed, thick, bed, fric, mask, before, after, out, S, PL, ST, RH = refs
    else:
        speed, thick, bed, fric, mask, halo, out, S, PL, ST, RH = refs
    levels, own_rows, cols = speed.shape
    lat = lax.axis_index("lat")
    window = ST.shape[1]
    planes = (thick, bed, fric, mask)
    S[:, 0:HALO, :] = jnp.zeros((levels, HALO, cols), F32)
    S[:, HALO + window :, :] = jnp.zeros((levels, HALO, cols), F32)
    PL[:, 0:HALO, :] = jnp.zeros((5, HALO, cols), F32)
    PL[:, HALO + window :, :] = jnp.zeros((5, HALO, cols), F32)

    def place(start, speeds, four):
        rows = pl.ds(pl.multiple_of(HALO + start, 8), speeds.shape[1])
        S[:, rows, :] = speeds
        for n in range(4):
            PL[n, rows, :] = four[n]

    own_four = [thick[...], bed[...], fric[...], mask[...].astype(F32)]
    if masked:
        own_at = HALO
        place(own_at, speed[...], own_four)
        place(0, *read_edge(before, levels))
        place(HALO + own_rows, *read_edge(after, levels))
    else:
        own_at = lat * HALO
        place(own_at, speed[...], own_four)
        place((1 - lat) * own_rows, *read_edge(halo, levels))
    tiles = range(window // 8)

    def rows_of(t):
        return slice(HALO + 8 * t, HALO + 8 * t + 8)

    sub = iota((8, cols), 0)
    top_row, bottom_row = sub == 0, sub == 7

    def north_of(ref, t, here):
        joined = jnp.where(top_row, ref[rows_of(t + 1)], here)
        return pltpu.roll(joined, 7, 0)

    def south_of(ref, t, here):
        joined = jnp.where(bottom_row, ref[rows_of(t - 1)], here)
        return pltpu.roll(joined, 1, 0)

    factor = 0.5 * 0.25 ** (-1.0 / 3.0)
    PL[4, HALO : HALO + window] = (
        PL[0, HALO : HALO + window] + PL[1, HALO : HALO + window]
    )
    for t in tiles:
        here = PL[4, rows_of(t)]
        PL[1, rows_of(t)] = (
            (-0.5 / factor)
            * PL[3, rows_of(t)]
            * PL[0, rows_of(t)]
            * (north_of(PL.at[4], t, here) - south_of(PL.at[4], t, here))
        )
        PL[2, rows_of(t)] = PL[2, rows_of(t)] * (1.0 / factor)
    if masked:
        count = lax.axis_size("lat")

        def inside(t):
            row = iota((8, cols), 0) + (8 * t - HALO)
            top = jnp.where(lat == 0, 0, -HALO)
            end = jnp.where(lat == count - 1, own_rows, own_rows + HALO)
            return jnp.logical_and(row >= top, row < end)

    def inverse_of(t):
        thickness = PL[0, rows_of(t)]
        if masked:
            thickness = jnp.where(inside(t), thickness, 1.0)
        return (levels - 1) / thickness

    def sweep(_, carry):
        for t in tiles:
            inverse = 0.5 * inverse_of(t)
            driving = PL[1, rows_of(t)]
            for k in range(levels):
                here = S[k, rows_of(t)]
                north, south = north_of(S.at[k], t, here), south_of(S.at[k], t, here)
                east, west = shift_lanes(here, 1), shift_lanes(here, -1)
                above = S[min(k + 1, levels - 1), rows_of(t)]
                below = S[max(k - 1, 0), rows_of(t)]
                by_level = (above - below) * inverse
                if k in (0, levels - 1):
                    by_level = 2.0 * by_level
                by_row = north - south
                by_col = east - west
                strain = (by_row * by_row + 4.0 * STRAIN_FLOOR) + (
                    0.25 * (by_col * by_col) + by_level * by_level
                )
                stiffness = jnp.exp2(jnp.log2(strain) * (-1.0 / 3.0))
                ST[k, 8 * t : 8 * t + 8] = stiffness
                RH[k, 8 * t : 8 * t + 8] = driving + stiffness * (
                    (north + south) + (east + west)
                )
        scale = [(0.5 * ASPECT) * inverse_of(t) * inverse_of(t) for t in tiles]
        upper, value, vertical, stiff, rest = {}, {}, {}, {}, {}
        for k in range(levels):
            for t in tiles:
                rows = slice(8 * t, 8 * t + 8)
                current = ST[0, rows] if k == 0 else stiff[t]
                partial = 4.0 * current
                right = RH[k, rows]
                if k == 0:
                    partial = partial + PL[2, rows_of(t)]
                else:
                    partial = partial + vertical[t] * rest[t]
                    right = right + vertical[t] * value[t]
                diagonal = partial
                if k < levels - 1:
                    stiff[t] = ST[k + 1, rows]
                    vertical[t] = scale[t] * (current + stiff[t])
                    diagonal = partial + vertical[t]
                invert = 1.0 / diagonal
                value[t] = right * invert
                RH[k, rows] = value[t]
                if k < levels - 1:
                    rest[t] = partial * invert
                    ST[k, rows] = vertical[t] * invert
        for k in range(levels - 1, -1, -1):
            for t in tiles:
                rows = slice(8 * t, 8 * t + 8)
                if k < levels - 1:
                    value[t] = RH[k, rows] + ST[k, rows] * value[t]
                fresh = value[t]
                if masked:
                    fresh = jnp.where(inside(t), fresh, 0.0)
                    value[t] = fresh
                S[k, rows_of(t)] = fresh
        return carry

    lax.fori_loop(0, SWEEPS, sweep, 0)
    for t in tiles:
        total = S[0, rows_of(t)]
        for k in range(1, levels):
            total = total + S[k, rows_of(t)]
        PL[4, rows_of(t)] = PL[0, rows_of(t)] * total * (1.0 / levels)
    for t in tiles:
        here = PL[4, rows_of(t)]
        change = north_of(PL.at[4], t, here) - south_of(PL.at[4], t, here)
        fresh = PL[0, rows_of(t)] - 0.25 * change
        PL[1, rows_of(t)] = PL[3, rows_of(t)] * fresh
    out[...] = PL[1, pl.ds(pl.multiple_of(HALO + own_at, 8), own_rows), :].astype(BF16)


def edge_rows(start, speed, thick, bed, fric, mask):
    levels, _, cols = speed.shape
    rows = pl.ds(start if isinstance(start, int) else pl.multiple_of(start, 8), HALO)
    parts = [speed[:, rows, :].reshape(levels * HALO, cols)]
    for plane in (thick, bed, fric):
        value = plane[rows, :]
        high = value.astype(BF16).astype(F32)
        parts += [high, value - high]
    parts += [mask[rows, :].astype(F32), jnp.zeros((HALO, cols), F32)]
    return jnp.concatenate(parts, 0).astype(BF16)


def read_edge(halo, levels):
    value = halo[...].astype(F32)
    planes = [value[(levels + n) * HALO : (levels + n + 1) * HALO] for n in range(7)]
    four = [planes[2 * n] + planes[2 * n + 1] for n in range(3)] + [planes[6]]
    return value[: levels * HALO].reshape(levels, HALO, value.shape[1]), four


def ice_load_of(speed, thick, bed, fric, mask, halos):
    levels, own_rows, cols = speed.shape
    window = own_rows + HALO * (1 if len(halos) == 1 else 2)
    return call(
        functools.partial(ice_kernel, masked=len(halos) != 1),
        "ice",
        pltpu.VMEM((own_rows, cols), BF16),
        (*leave(speed, thick, bed, fric, mask), *keep(*halos)),
        [
            pltpu.VMEM((levels, window + 2 * HALO, cols), F32),
            pltpu.VMEM((5, window + 2 * HALO, cols), F32),
            pltpu.VMEM((levels, window, cols), F32),
            pltpu.VMEM((levels, window, cols), F32),
        ],
    )


def stencil_tables():
    pick_row = np.zeros((32 * COMPS, 24), np.float32)
    pick_col = np.zeros((4, 24, 3 * VEC), np.float32)
    keep = np.zeros((4, 32 * COMPS, 3 * VEC), np.float32)
    for c in range(COMPS):
        for p in range(2):
            for s in range(2):
                for q in range(2):
                    for layer in range(LAYERS):
                        m = ((c * 2 + p) * 2 + s) * PAIR + q * LAYERS + layer
                        pick_row[m, 3 * (4 * p + 2 * q + s) + c] = 1.0
                        for dj in range(3):
                            for c2 in range(COMPS):
                                for q2 in range(2):
                                    for l2 in range(LAYERS):
                                        n = dj * VEC + c2 * PAIR + q2 * LAYERS + l2
                                        p2 = l2 - layer + p
                                        s2 = dj - 1 + s
                                        if p2 in (0, 1) and s2 in (0, 1):
                                            keep[2 * p2 + s2, m, n] = 1.0
    for p2 in range(2):
        for s2 in range(2):
            for dj in range(3):
                for c2 in range(COMPS):
                    for q2 in range(2):
                        for l2 in range(LAYERS):
                            n = dj * VEC + c2 * PAIR + q2 * LAYERS + l2
                            pick_col[2 * p2 + s2, 3 * (4 * p2 + 2 * q2 + s2) + c2, n] = 1.0
    return pick_row, pick_col, keep


def stencil_kernel(matrix, pick_row, pick_col, keep, out, theta):
    exact = functools.partial(
        jnp.dot, precision=lax.Precision.HIGHEST, preferred_element_type=F32
    )
    entries = matrix[...]
    rows = exact(pick_row[...], entries)
    full = jnp.zeros((rows.shape[0], 3 * VEC), F32)
    for n in range(4):
        full = full + keep[n] * exact(rows, pick_col[n])
    high = full.astype(BF16).astype(F32)
    low = full - high
    blank = jnp.zeros((rows.shape[0], PAIR), F32)
    parts = []
    for dj in range(3):
        cut = slice(dj * VEC, (dj + 1) * VEC)
        parts += [high[:, cut], high[:, cut], low[:, cut], blank]
    out[...] = jnp.concatenate(parts, 1).astype(BF16)
    square = iota(entries.shape, 0) == iota(entries.shape, 1)
    trace = jnp.sum(jnp.where(square, entries, 0.0), keepdims=True)
    theta[...] = jnp.broadcast_to(trace * (8.0 * TYPICAL_MODULUS / 24.0), (8, 128))


def stencil_of(matrix):
    tables = [jnp.asarray(t) for t in stencil_tables()]
    return call(
        stencil_kernel,
        "stencil",
        (
            pltpu.VMEM((32 * COMPS, 3 * (3 * VEC + PAIR)), BF16),
            pltpu.VMEM((8, 128), F32),
        ),
        leave(matrix, *tables),
    )


def pack_kernel(*refs, map_rows, masked):
    ice, (disp, shear, visc, index, weight) = refs[:5], refs[5:10]
    low, high = refs[10:12]
    edges, TS = refs[12:-1], refs[-1]
    layers = shear.shape[0]
    count = COMPS * layers
    spot = index[...]
    TS[0:4, 0 : 2 * HALO] = ((spot % 2) * map_rows + spot // 2).astype(F32)
    TS[4:8, 0 : 2 * HALO] = weight[...]
    table = jnp.transpose(TS[...])
    for n, out in enumerate((low, high)):
        rows = slice(n * HALO, (n + 1) * HALO)
        for c in range(COMPS):
            for k in range(layers):
                out[c * layers + k] = disp[c, k, rows]
        for k in range(layers):
            out[count + k] = shear[k, rows]
            out[count + layers + k] = visc[k, rows]
        out[count + 2 * layers, :, 0:8] = table[rows]
    top = ice[0].shape[1] - HALO
    if masked:
        edges[0][...] = edge_rows(0, *ice)
        edges[1][...] = edge_rows(top, *ice)
    else:
        edges[0][...] = edge_rows(jnp.where(lax.axis_index("lat") == 0, top, 0), *ice)


def region_kernel(north, low, high, south, out):
    for n, piece in enumerate((north, low, high, south)):
        out[:, n * HALO : (n + 1) * HALO] = piece[...]


def at(base, size, index):
    return base.at[pl.ds(index * size, size)]


def element_force(vector, stencil, coef):
    high = vector.astype(BF16).astype(F32)
    split = jnp.concatenate([high, vector - high], 0).astype(BF16)
    parts = []
    for moved in (shift_lanes(split, -1), split, shift_lanes(split, 1)):
        parts += [moved, moved[: VEC + PAIR]]
    force = jnp.dot(stencil, jnp.concatenate(parts, 0), preferred_element_type=F32)
    sums = []
    for c in range(COMPS):
        total = None
        for n in range(4):
            first = (c * 4 + n) * PAIR
            piece = force[first : first + PAIR] * coef[n * PAIR : (n + 1) * PAIR]
            total = piece if total is None else total + piece
        sums.append(total)
    return sums


def apply_rows(source, coefs, stencil, start, stop, store):
    weights = stencil[...]
    front = iota((PAIR, source.shape[1]), 0) < LAYERS
    forces = {}
    for pair in range(start - 1, stop + 1):
        forces[pair] = element_force(
            at(source, VEC, pair)[...], weights, at(coefs, 4 * PAIR, pair)[...]
        )
        done = pair - 1
        if done >= start:
            sums = []
            for c in range(COMPS):
                swapped = jnp.where(front, forces[pair][c], forces[done - 1][c])
                sums.append(forces[done][c] + pltpu.roll(swapped, LAYERS, 0))
            store(done, sums)
            del forces[done - 1]


def domain_of(own_rows, cols):
    shell = (lax.axis_size("group") - 1) * own_rows
    base = iota((PAIR, 128), 0) // LAYERS + lax.axis_index("group") * own_rows

    def mask(pair):
        offset = pair - 1 - HALO
        live = jnp.logical_and(base >= -offset, base < shell - offset)
        one = jnp.where(live, 1.0, 0.0)
        return jnp.concatenate([one] * (cols // 128), 1)

    return mask


def relax_kernel(*refs, pieces):
    E = refs[:pieces]
    stencil, theta = refs[pieces : pieces + 2]
    r_out, c_out, x_out, lw_out, ut_out = refs[pieces + 2 : pieces + 7]
    XP, CR, XS, SH, VI = refs[pieces + 7 :]
    group, lat, rad = (lax.axis_index(n) for n in ("group", "lat", "rad"))
    lat_count = lax.axis_size("lat")
    rows, width = E[0].shape[-2:]
    own_rows = rows - 2 * HALO
    cols = XP.shape[1]
    rad_layers = LAYERS // 2
    planes = COMPS * rad_layers

    def block(lb, rb, plane):
        if pieces == 1:
            return E[0][lb * 2 + rb, plane]
        near, far = [
            jnp.where(rad == rb, E[n][plane], E[n + 1][plane]) for n in (0, 2)
        ]
        return jnp.where(lat == lb, near, far)

    for lb in range(lat_count):
        for rb in range(2):
            for k in range(rad_layers):
                layer = rb * rad_layers + k
                for c in range(COMPS):
                    value = block(lb, rb, c * rad_layers + k)
                    for q in range(2):
                        first = (1 - q) * VEC + c * PAIR + q * LAYERS + layer
                        XS[lb, pl.ds(first, rows, VEC), :] = value
                for ref, plane in ((SH, planes + k), (VI, planes + rad_layers + k)):
                    value = block(lb, rb, plane)
                    for q in range(2):
                        first = (1 - q) * PAIR + q * LAYERS + layer
                        ref[lb, pl.ds(first, rows, PAIR), :] = value

    mask = domain_of(own_rows, cols)
    layer8 = iota((PAIR, cols), 0) % LAYERS
    top_layer, last_layer = layer8 == 0, layer8 == LAYERS - 1
    shrink = 1.0 / theta[0:1, 0:1]
    eighth = 0.125 * shrink

    def corner_means(nodal, scale):
        both = nodal + pltpu.roll(nodal, LAYERS, 0)
        up = jnp.where(last_layer, 0.0, pltpu.roll(both, PAIR - 1, 0))
        down = jnp.where(top_layer, 0.0, pltpu.roll(both, 1, 0))
        result = []
        for side in (both + up, both + down):
            side = scale * side
            for step in (1, -1):
                result.append(side + shift_lanes(side, step))
        return jnp.concatenate(result, 0)

    for pair in range(4, 29):
        domain = mask(pair)
        shear, viscosity, vector = [
            jnp.concatenate([at(ref.at[lb], size, pair)[...] for lb in range(lat_count)], 1)
            for ref, size in ((SH, PAIR), (VI, PAIR), (XS, VEC))
        ]
        ratio = shear / viscosity
        damp = 1.0 / (1.0 + ratio)
        modulus = domain * shear * damp
        relaxed = modulus * ratio * damp
        at(c_out, 4 * PAIR, pair)[...] = corner_means(modulus, eighth)
        at(CR, 4 * PAIR, pair)[...] = corner_means(relaxed, 0.125)
        at(XP, VEC, pair)[...] = vector * jnp.concatenate([domain] * COMPS, 0)

    def store(pair, sums):
        domain = mask(pair)
        at(r_out, VEC, pair)[...] = jnp.concatenate([-domain * x for x in sums], 0)

    apply_rows(XP, CR, stencil, 5, 28, store)
    for t in range(own_rows // 2):
        x_out[t * VEC : (t + 1) * VEC] = at(XP, VEC, HALO + 1 + 2 * t)[...]

    blocks = lw_out.shape[2] // 3
    map_rows = blocks // 2
    tile_rows = map_rows // lat_count
    row = iota((rows, 1), 0) - HALO + group * own_rows
    shell = (lax.axis_size("group") - 1) * own_rows
    scale = jnp.where(jnp.logical_and(row >= 0, row < shell), -LOAD_SCALE, 0.0)
    own = slice(HALO, HALO + own_rows)
    for lb in range(lat_count):
        table = block(lb, 0, planes + 2 * rad_layers)
        spots = iota((rows, blocks), 1).astype(F32)
        own_spots = iota((own_rows, 128), 1).astype(F32)
        loads = jnp.zeros((rows, blocks), F32)
        lift = jnp.zeros((own_rows, 128), F32)
        for k in range(4):
            index, weight = table[:, k : k + 1], table[:, 4 + k : 5 + k]
            loads = loads + jnp.where(spots == index, weight, 0.0)
            right = index[own] >= map_rows
            near = index[own] - jnp.where(right, map_rows, 0) - (lat * tile_rows).astype(F32)
            here = jnp.logical_and(near >= 0, near < tile_rows)
            spot = jnp.where(here, near + jnp.where(right, tile_rows, 0), -1.0)
            lift = lift + jnp.where(own_spots == spot, weight[own], 0.0)
        loads = loads * scale
        high = loads.astype(BF16).astype(F32)
        middle = (loads - high).astype(BF16).astype(F32)
        low = loads - high - middle
        lw_out[lb] = jnp.concatenate([high, middle, low], 1).astype(BF16)
        lift = lift * (1.0 / LAYERS)
        for layer in range(LAYERS):
            first = lb * own_rows * LAYERS + layer
            ut_out[pl.ds(first, own_rows, LAYERS), :] = lift


def krylov_kernel(*refs, loads):
    load_refs = refs[:loads]
    stencil, r_in, coefs, x_own, lw, ut = refs[loads : loads + 6]
    payload, v_out = refs[loads + 6 : loads + 8]
    V, TOP = refs[loads + 8 :]
    lat = lax.axis_index("lat")
    lat_count = lax.axis_size("lat")
    cols = r_in.shape[1]
    width = cols // lat_count
    pairs = x_own.shape[0] // VEC
    own_rows = 2 * pairs
    if loads == 2:
        own, other = load_refs[0][...], load_refs[1][...]
        own, other = own.astype(F32), other.astype(F32)
        tiles = [jnp.where(lat == 0, own, other), jnp.where(lat == 0, other, own)]
        field = jnp.concatenate(tiles, 0)
    else:
        field = load_refs[0][...].astype(F32)
    half = field.shape[1] // 2
    blocks = jnp.concatenate([field[:, :half], field[:, half:]], 0)
    blocks = jnp.concatenate([blocks] * 3, 0).astype(BF16)
    for lb in range(lat_count):
        TOP[lb] = jnp.zeros(TOP.shape[1:], F32)
        top = jnp.dot(lw[lb], blocks, preferred_element_type=F32)
        for q in range(2):
            TOP[lb, pl.ds((1 - q) * PAIR + q * LAYERS, top.shape[0], PAIR), :] = top
    for pair in range(5, 28):
        vector = at(r_in, VEC, pair)[...]
        top = [at(TOP.at[lb], PAIR, pair)[...] for lb in range(lat_count)]
        upright = vector[2 * PAIR :] + jnp.concatenate(top, 1)
        at(V.at[0], VEC, pair)[...] = jnp.concatenate([vector[: 2 * PAIR], upright], 0)
    mask = domain_of(own_rows, cols)
    for n in range(ITERS):

        def store(pair, sums, n=n):
            domain = mask(pair)
            fresh = jnp.concatenate([domain * x for x in sums], 0)
            at(V.at[n + 1], VEC, pair)[...] = fresh - at(V.at[n], VEC, pair)[...]

        apply_rows(V.at[n], coefs, stencil, 6 + n, 27 - n, store)

    own_pairs = [HALO + 1 + 2 * t for t in range(pairs)]
    sums = [None] * (2 * ITERS)
    for pair in own_pairs:
        values = [at(V.at[n], VEC, pair)[...] for n in range(ITERS + 1)]
        for k in range(2 * ITERS):
            product = values[k // 2] * values[(k + 1) // 2]
            for r in range(COMPS):
                for c in range(cols // 128):
                    piece = product[PAIR * r : PAIR * r + PAIR, 128 * c : 128 * c + 128]
                    sums[k] = piece if sums[k] is None else sums[k] + piece
    for k in range(2 * ITERS):
        payload[k : k + 1] = jnp.sum(sums[k], 0, keepdims=True)
    fields = []
    upright = slice(2 * PAIR, VEC)
    for lb in range(lat_count):
        lanes = slice(lb * width, (lb + 1) * width)
        row = [[x_own[t * VEC + 2 * PAIR : (t + 1) * VEC, lanes] for t in range(pairs)]]
        for n in range(ITERS):
            row.append([at(V.at[n], VEC, pair)[upright, lanes] for pair in own_pairs])
        fields.append(jnp.concatenate([jnp.concatenate(x, 0) for x in row], 1))
    fields = jnp.concatenate(fields, 0)
    spots = (payload.shape[0] - 2 * ITERS) // (ITERS + 1)
    lift = lax.dot_general(
        ut[...],
        fields,
        (((0,), (0,)), ((), ())),
        precision=lax.Precision.HIGHEST,
        preferred_element_type=F32,
    )
    for n in range(ITERS + 1):
        payload[2 * ITERS + n * spots : 2 * ITERS + (n + 1) * spots] = lift[
            :spots, n * width : (n + 1) * width
        ]
    own = pl.ds(pl.multiple_of(lat * width, 128), width)
    for n in range(ITERS):
        for t, pair in enumerate(own_pairs):
            v_out[n, t * VEC : (t + 1) * VEC] = V[n, pair * VEC : (pair + 1) * VEC, own]
    v_out[ITERS] = x_own[:, own]


def finish_kernel(payload, theta, v, bed, disp_out, bed_out, X):
    rad = lax.axis_index("rad")
    moment = [
        jnp.broadcast_to(jnp.sum(payload[k : k + 1], 1, keepdims=True), (8, 128))
        for k in range(2 * ITERS)
    ]

    def product(left, right, size=False):
        by_degree = {}
        for i, a in enumerate(left):
            for j, b in enumerate(right):
                term = a * b
                if size:
                    term = jnp.abs(term)
                by_degree[i + j] = by_degree[i + j] + term if i + j in by_degree else term
        total = None
        for k, weight in by_degree.items():
            term = weight * (jnp.abs(moment[k]) if size else moment[k])
            total = term if total is None else total + term
        return total

    def shifted(poly):
        result = list(poly) + [jnp.zeros((8, 128), F32)]
        for i, a in enumerate(poly):
            result[i + 1] = result[i + 1] + a
        return result

    one, zero = jnp.ones((8, 128), F32), jnp.zeros((8, 128), F32)
    residual, direction, answer = [one], [one], [zero] * ITERS
    norm = moment[0]
    live = None
    for n in range(ITERS):
        image = shifted(direction)
        step = norm / product(direction, image)
        if live is not None:
            step = jnp.where(live, step, 0.0)
        for i, a in enumerate(direction):
            answer[i] = answer[i] + step * a
        if n == ITERS - 1:
            break
        residual = [
            (residual[i] if i < len(residual) else zero) - step * a for i, a in enumerate(image)
        ]
        fresh = product(residual, residual)
        above = fresh > 1e-7 * product(residual, residual, True)
        live = above if live is None else jnp.logical_and(live, above)
        ratio = jnp.where(live, fresh / norm, 0.0)
        direction = [
            a + (ratio * direction[i] if i < len(direction) else zero)
            for i, a in enumerate(residual)
        ]
        norm = jnp.where(live, fresh, 1.0)
    raw = [a[0:1] for a in answer]
    answer = [a / theta[0:1] for a in raw]
    total = v[ITERS]
    for n in range(ITERS):
        total = total + answer[n] * v[n]
    X[...] = total
    layers = disp_out.shape[1]
    pairs = disp_out.shape[2] // 2
    for c in range(COMPS):
        for k in range(layers):
            for q in range(2):
                lower = X[pl.ds(c * PAIR + q * LAYERS + k, pairs, VEC), :]
                upper = X[pl.ds(c * PAIR + q * LAYERS + layers + k, pairs, VEC), :]
                disp_out[c, k, pl.ds(q, pairs, 2), :] = jnp.where(rad == 0, lower, upper)
    rows, cols = bed.shape
    spots = 2 * rows
    base = 2 * ITERS
    lift = payload[base : base + spots]
    for n in range(ITERS):
        lift = lift + answer[n] * payload[base + (n + 1) * spots : base + (n + 2) * spots]
    for h in range(2):
        lanes = slice(h * cols // 2, (h + 1) * cols // 2)
        bed_out[:, lanes] = bed[:, lanes] + UPLIFT_SCALE * lift[h * rows : (h + 1) * rows]


def per_device(
    displacement_prev,
    shear_modulus,
    viscosity,
    element_matrix,
    regrid_index,
    regrid_weight,
    ice_thickness,
    bed_elevation,
    basal_friction,
    ice_mask,
    speed_guess,
):
    groups, lats = lax.axis_size("group"), lax.axis_size("lat")
    rad_layers, own_rows, width = shear_modulus.shape
    tile_rows, map_cols = ice_thickness.shape
    cols = lats * width
    blocks = 2 * tile_rows * lats
    planes = COMPS * rad_layers + 2 * rad_layers + 1
    ice_args = (speed_guess, ice_thickness, bed_elevation, basal_friction, ice_mask)

    levels = speed_guess.shape[0]
    low, high, *edges = call(
        functools.partial(pack_kernel, map_rows=tile_rows * lats, masked=lats != 2),
        "pack",
        (pltpu.VMEM((planes, HALO, width), F32),) * 2
        + (pltpu.VMEM(((levels + 8) * HALO, map_cols), BF16),) * (1 if lats == 2 else 2),
        leave(
            *ice_args,
            displacement_prev,
            shear_modulus,
            viscosity,
            regrid_index[:, 0].T,
            regrid_weight[:, 0].T,
        ),
        [pltpu.VMEM((8, 128), F32)],
    )
    north = lax.ppermute(high, "group", [(i, (i + 1) % groups) for i in range(groups)])
    south = lax.ppermute(low, "group", [(i, (i - 1) % groups) for i in range(groups)])
    if lats == 2:
        halos = [lax.ppermute(edges[0], "lat", [(0, 1), (1, 0)])]
    else:
        halos = [
            lax.ppermute(edges[1], "lat", [(i, i + 1) for i in range(lats - 1)]),
            lax.ppermute(edges[0], "lat", [(i + 1, i) for i in range(lats - 1)]),
        ]
    stencil, theta = stencil_of(element_matrix)
    north, south, halos = lax.optimization_barrier((north, south, halos))
    region = call(
        region_kernel,
        "region",
        pltpu.VMEM((planes, 2 * own_rows, width), F32),
        keep(north, low, high, south),
    )
    if lats == 2:
        far = lax.ppermute(region, "lat", [(0, 1), (1, 0)])
        near = lax.ppermute(region, "rad", [(0, 1), (1, 0)])
        ice_load = ice_load_of(*ice_args, halos)
        far, ice_load = lax.optimization_barrier((far, ice_load))
        pieces = [region, near, far, lax.ppermute(far, "rad", [(0, 1), (1, 0)])]
    else:
        pieces = [lax.all_gather(region, ("lat", "rad"))]
        ice_load = ice_load_of(*ice_args, halos)
    if lats == 2:
        loads = [ice_load, lax.ppermute(ice_load, "lat", [(0, 1), (1, 0)])]
    else:
        loads = [lax.all_gather(ice_load, "lat", axis=0, tiled=True)]
    pairs = own_rows // 2
    r_start, coefs, x_own, lw, ut = call(
        functools.partial(relax_kernel, pieces=len(pieces)),
        "relax",
        (
            pltpu.VMEM((33 * VEC, cols), F32),
            pltpu.VMEM((33 * 4 * PAIR, cols), F32),
            pltpu.VMEM((pairs * VEC, cols), F32),
            pltpu.VMEM((lats, 2 * own_rows, 3 * blocks), BF16),
            pltpu.VMEM((lats * own_rows * LAYERS, 128), F32),
        ),
        keep(*pieces, stencil, theta),
        [
            pltpu.VMEM((33 * VEC, cols), F32),
            pltpu.VMEM((33 * 4 * PAIR, cols), F32),
            pltpu.VMEM((lats, 33 * VEC, width), F32),
            pltpu.VMEM((lats, 33 * PAIR, width), F32),
            pltpu.VMEM((lats, 33 * PAIR, width), F32),
        ],
    )
    spots = 2 * tile_rows
    payload, vectors = call(
        functools.partial(krylov_kernel, loads=len(loads)),
        "krylov",
        (
            pltpu.VMEM((2 * ITERS + (ITERS + 1) * spots, width), F32),
            pltpu.VMEM((ITERS + 1, pairs * VEC, width), F32),
        ),
        keep(*loads, stencil, r_start, coefs, x_own, lw, ut),
        [
            pltpu.VMEM((ITERS + 1, 33 * VEC, cols), F32),
            pltpu.VMEM((lats, 33 * PAIR, width), F32),
        ],
    )
    step = 1
    while step < groups:
        payload = payload + lax.ppermute(
            payload, "group", [(i, i ^ step) for i in range(groups)]
        )
        step *= 2
    return call(
        finish_kernel,
        "finish",
        (
            jax.ShapeDtypeStruct((COMPS, rad_layers, own_rows, width), F32),
            jax.ShapeDtypeStruct((tile_rows, map_cols), F32),
        ),
        (*keep(payload, theta, vectors), bed_elevation),
        [pltpu.VMEM((pairs * VEC, width), F32)],
    )


def solution(mesh):
    in_specs = (
        P(None, "rad", "group", "lat"),
        P("rad", "group", "lat"),
        P("rad", "group", "lat"),
        P(),
        P("group", "lat", None),
        P("group", "lat", None),
        P("lat", None),
        P("lat", None),
        P("lat", None),
        P("lat", None),
        P(None, "lat", None),
    )
    out_specs = (P(None, "rad", "group", "lat"), P("lat", None))
    return jax.shard_map(
        per_device, mesh=mesh, in_specs=in_specs, out_specs=out_specs, check_vma=False
    )
```

```python
import functools

import jax
import jax.numpy as jnp
import numpy as np
from jax import lax
from jax.experimental import pallas as pl
from jax.experimental.pallas import tpu as pltpu
from jax.sharding import PartitionSpec as P

SWEEPS = 6
ITERS = 4
HALO = 8
COMPS = 3
LAYERS = 4
PAIR = 2 * LAYERS
VEC = COMPS * PAIR
LOAD_SCALE = 20.0
UPLIFT_SCALE = 0.5
ASPECT = 0.01
STRAIN_FLOOR = 0.01
TYPICAL_MODULUS = 2.2

F32 = jnp.float32
BF16 = jnp.bfloat16


def vmem():
    return pl.BlockSpec(memory_space=pltpu.VMEM)


def keep(*arrays):
    return [pltpu.with_memory_space_constraint(a, pltpu.VMEM) for a in arrays]


def leave(*arrays):
    return [pltpu.with_memory_space_constraint(a, pltpu.HBM) for a in arrays]


def call(body, out, inputs, scratch=(), specs=None):
    lats = lax.axis_size("lat")
    return pl.pallas_call(
        body,
        out_shape=out,
        in_specs=specs or [vmem()] * len(inputs),
        out_specs=jax.tree.map(lambda _: vmem(), out),
        scratch_shapes=list(scratch),
        compiler_params=pltpu.CompilerParams(vmem_limit_bytes=(8 if lats == 2 else 40) << 20),
    )(*inputs)


def iota(shape, dim):
    return lax.broadcasted_iota(jnp.int32, shape, dim)


def shift_lanes(x, step):
    zero = jnp.zeros((x.shape[0], 1), x.dtype)
    if step == 1:
        return jnp.concatenate([x[:, 1:], zero], 1)
    return jnp.concatenate([zero, x[:, :-1]], 1)


def ice_kernel(*refs, masked):
    if masked:
        speed, thick, bed, fric, mask, before, after, out, S, PL, ST, RH = refs
    else:
        speed, thick, bed, fric, mask, halo, out, S, PL, ST, RH = refs
    levels, own_rows, cols = speed.shape
    lat = lax.axis_index("lat")
    window = ST.shape[1]
    S[:, 0:HALO, :] = jnp.zeros((levels, HALO, cols), F32)
    S[:, HALO + window :, :] = jnp.zeros((levels, HALO, cols), F32)
    PL[:, 0:HALO, :] = jnp.zeros((5, HALO, cols), F32)
    PL[:, HALO + window :, :] = jnp.zeros((5, HALO, cols), F32)

    def place(start, speeds, four):
        rows = pl.ds(pl.multiple_of(HALO + start, 8), speeds.shape[1])
        S[:, rows, :] = speeds
        for n in range(4):
            PL[n, rows, :] = four[n]

    own_four = [thick[...], bed[...], fric[...], mask[...]]
    if masked:
        own_at = HALO
        place(own_at, speed[...], own_four)
        place(0, *read_edge(before, levels))
        place(HALO + own_rows, *read_edge(after, levels))
    else:
        own_at = lat * HALO
        place(own_at, speed[...], own_four)
        place((1 - lat) * own_rows, *read_edge(halo, levels))
    tiles = range(window // 8)

    def rows_of(t):
        return slice(HALO + 8 * t, HALO + 8 * t + 8)

    sub = iota((8, cols), 0)
    top_row, bottom_row = sub == 0, sub == 7

    def north_of(ref, t, here):
        joined = jnp.where(top_row, ref[rows_of(t + 1)], here)
        return pltpu.roll(joined, 7, 0)

    def south_of(ref, t, here):
        joined = jnp.where(bottom_row, ref[rows_of(t - 1)], here)
        return pltpu.roll(joined, 1, 0)

    factor = 0.5 * 0.25 ** (-1.0 / 3.0)
    PL[4, HALO : HALO + window] = (
        PL[0, HALO : HALO + window] + PL[1, HALO : HALO + window]
    )
    for t in tiles:
        here = PL[4, rows_of(t)]
        PL[1, rows_of(t)] = (
            (-0.5 / factor)
            * PL[3, rows_of(t)]
            * PL[0, rows_of(t)]
            * (north_of(PL.at[4], t, here) - south_of(PL.at[4], t, here))
        )
        PL[2, rows_of(t)] = PL[2, rows_of(t)] * (1.0 / factor)
    if masked:
        count = lax.axis_size("lat")

        def inside(t):
            row = iota((8, cols), 0) + (8 * t - HALO)
            top = jnp.where(lat == 0, 0, -HALO)
            end = jnp.where(lat == count - 1, own_rows, own_rows + HALO)
            return jnp.logical_and(row >= top, row < end)

    def inverse_of(t):
        thickness = PL[0, rows_of(t)]
        if masked:
            thickness = jnp.where(inside(t), thickness, 1.0)
        return (levels - 1) / thickness

    def sweep(_, carry):
        for t in tiles:
            inverse = 0.5 * inverse_of(t)
            driving = PL[1, rows_of(t)]
            for k in range(levels):
                here = S[k, rows_of(t)]
                north, south = north_of(S.at[k], t, here), south_of(S.at[k], t, here)
                east, west = shift_lanes(here, 1), shift_lanes(here, -1)
                above = S[min(k + 1, levels - 1), rows_of(t)]
                below = S[max(k - 1, 0), rows_of(t)]
                by_level = (above - below) * inverse
                if k in (0, levels - 1):
                    by_level = 2.0 * by_level
                by_row = north - south
                by_col = east - west
                strain = (by_row * by_row + 4.0 * STRAIN_FLOOR) + (
                    0.25 * (by_col * by_col) + by_level * by_level
                )
                stiffness = jnp.exp2(jnp.log2(strain) * (-1.0 / 3.0))
                ST[k, 8 * t : 8 * t + 8] = stiffness
                RH[k, 8 * t : 8 * t + 8] = driving + stiffness * (
                    (north + south) + (east + west)
                )
        scale = [(0.5 * ASPECT) * inverse_of(t) * inverse_of(t) for t in tiles]
        value, vertical, stiff, rest = {}, {}, {}, {}
        for k in range(levels):
            for t in tiles:
                rows = slice(8 * t, 8 * t + 8)
                current = ST[0, rows] if k == 0 else stiff[t]
                partial = 4.0 * current
                right = RH[k, rows]
                if k == 0:
                    partial = partial + PL[2, rows_of(t)]
                else:
                    partial = partial + vertical[t] * rest[t]
                    right = right + vertical[t] * value[t]
                diagonal = partial
                if k < levels - 1:
                    stiff[t] = ST[k + 1, rows]
                    vertical[t] = scale[t] * (current + stiff[t])
                    diagonal = partial + vertical[t]
                invert = 1.0 / diagonal
                value[t] = right * invert
                RH[k, rows] = value[t]
                if k < levels - 1:
                    rest[t] = partial * invert
                    ST[k, rows] = vertical[t] * invert
        for k in range(levels - 1, -1, -1):
            for t in tiles:
                rows = slice(8 * t, 8 * t + 8)
                if k < levels - 1:
                    value[t] = RH[k, rows] + ST[k, rows] * value[t]
                fresh = value[t]
                if masked:
                    fresh = jnp.where(inside(t), fresh, 0.0)
                    value[t] = fresh
                S[k, rows_of(t)] = fresh
        return carry

    lax.fori_loop(0, SWEEPS, sweep, 0)
    for t in tiles:
        total = S[0, rows_of(t)]
        for k in range(1, levels):
            total = total + S[k, rows_of(t)]
        PL[4, rows_of(t)] = PL[0, rows_of(t)] * total * (1.0 / levels)
    for t in tiles:
        here = PL[4, rows_of(t)]
        change = north_of(PL.at[4], t, here) - south_of(PL.at[4], t, here)
        fresh = PL[0, rows_of(t)] - 0.25 * change
        PL[1, rows_of(t)] = PL[3, rows_of(t)] * fresh
    out[...] = PL[1, pl.ds(pl.multiple_of(HALO + own_at, 8), own_rows), :].astype(BF16)


def edge_rows(start, speed, thick, bed, fric, mask):
    levels, _, cols = speed.shape
    rows = pl.ds(start if isinstance(start, int) else pl.multiple_of(start, 8), HALO)
    parts = [speed[:, rows, :].reshape(levels * HALO, cols)]
    for plane in (thick, bed, fric):
        value = plane[rows, :]
        high = value.astype(BF16).astype(F32)
        parts += [high, value - high]
    parts += [mask[rows, :].astype(F32), jnp.zeros((HALO, cols), F32)]
    return jnp.concatenate(parts, 0).astype(BF16)


def read_edge(halo, levels):
    value = halo[...].astype(F32)
    planes = [value[(levels + n) * HALO : (levels + n + 1) * HALO] for n in range(7)]
    four = [planes[2 * n] + planes[2 * n + 1] for n in range(3)] + [planes[6]]
    return value[: levels * HALO].reshape(levels, HALO, value.shape[1]), four


def ice_load_of(speed, thick, bed, fric, mask, halos):
    levels, own_rows, cols = speed.shape
    window = own_rows + HALO * (1 if len(halos) == 1 else 2)
    return call(
        functools.partial(ice_kernel, masked=len(halos) != 1),
        pltpu.VMEM((own_rows, cols), BF16),
        keep(speed, thick, bed, fric, mask, *halos),
        [
            pltpu.VMEM((levels, window + 2 * HALO, cols), F32),
            pltpu.VMEM((5, window + 2 * HALO, cols), F32),
            pltpu.VMEM((levels, window, cols), F32),
            pltpu.VMEM((levels, window, cols), F32),
        ],
    )


def stencil_tables():
    pick_row = np.zeros((32 * COMPS, 24), np.float32)
    pick_col = np.zeros((4, 24, 3 * VEC), np.float32)
    keep = np.zeros((4, 32 * COMPS, 3 * VEC), np.float32)
    for c in range(COMPS):
        for p in range(2):
            for s in range(2):
                for q in range(2):
                    for layer in range(LAYERS):
                        m = ((c * 2 + p) * 2 + s) * PAIR + q * LAYERS + layer
                        pick_row[m, 3 * (4 * p + 2 * q + s) + c] = 1.0
                        for dj in range(3):
                            for c2 in range(COMPS):
                                for q2 in range(2):
                                    for l2 in range(LAYERS):
                                        n = dj * VEC + c2 * PAIR + q2 * LAYERS + l2
                                        p2 = l2 - layer + p
                                        s2 = dj - 1 + s
                                        if p2 in (0, 1) and s2 in (0, 1):
                                            keep[2 * p2 + s2, m, n] = 1.0
    for p2 in range(2):
        for s2 in range(2):
            for dj in range(3):
                for c2 in range(COMPS):
                    for q2 in range(2):
                        for l2 in range(LAYERS):
                            n = dj * VEC + c2 * PAIR + q2 * LAYERS + l2
                            pick_col[2 * p2 + s2, 3 * (4 * p2 + 2 * q2 + s2) + c2, n] = 1.0
    return pick_row, pick_col, keep


def stencil_kernel(matrix, pick_row, pick_col, keep, out, theta):
    exact = functools.partial(
        jnp.dot, precision=lax.Precision.HIGHEST, preferred_element_type=F32
    )
    entries = matrix[...]
    rows = exact(pick_row[...], entries)
    full = jnp.zeros((rows.shape[0], 3 * VEC), F32)
    for n in range(4):
        full = full + keep[n] * exact(rows, pick_col[n])
    high = full.astype(BF16).astype(F32)
    low = full - high
    blank = jnp.zeros((rows.shape[0], PAIR), F32)
    parts = []
    for dj in range(3):
        cut = slice(dj * VEC, (dj + 1) * VEC)
        parts += [high[:, cut], high[:, cut], low[:, cut], blank]
    out[...] = jnp.concatenate(parts, 1).astype(BF16)
    square = iota(entries.shape, 0) == iota(entries.shape, 1)
    trace = jnp.sum(jnp.where(square, entries, 0.0), keepdims=True)
    theta[...] = jnp.broadcast_to(trace * (8.0 * TYPICAL_MODULUS / 24.0), (8, 128))


def stencil_of(matrix):
    tables = [jnp.asarray(t) for t in stencil_tables()]
    return call(
        stencil_kernel,
        (
            pltpu.VMEM((32 * COMPS, 3 * (3 * VEC + PAIR)), BF16),
            pltpu.VMEM((8, 128), F32),
        ),
        leave(matrix, *tables),
    )


def pack_kernel(*refs, map_rows, masked):
    ice, (disp, shear, visc, index, weight) = refs[:5], refs[5:10]
    low, high = refs[10:12]
    copies = refs[12:17]
    edges, TS = refs[17:-1], refs[-1]
    for source, copy in zip(ice, copies):
        copy[...] = source[...].astype(F32)
    layers = shear.shape[0]
    count = COMPS * layers
    spot = index[...]
    TS[0:4, 0 : 2 * HALO] = ((spot % 2) * map_rows + spot // 2).astype(F32)
    TS[4:8, 0 : 2 * HALO] = weight[...]
    table = jnp.transpose(TS[...])
    for n, out in enumerate((low, high)):
        rows = slice(n * HALO, (n + 1) * HALO)
        for c in range(COMPS):
            for k in range(layers):
                out[c * layers + k] = disp[c, k, rows]
        for k in range(layers):
            out[count + k] = shear[k, rows]
            out[count + layers + k] = visc[k, rows]
        out[count + 2 * layers, :, 0:8] = table[rows]
    top = ice[0].shape[1] - HALO
    if masked:
        edges[0][...] = edge_rows(0, *ice)
        edges[1][...] = edge_rows(top, *ice)
    else:
        edges[0][...] = edge_rows(jnp.where(lax.axis_index("lat") == 0, top, 0), *ice)


def region_kernel(*pieces):
    out = pieces[-1]
    for n, piece in enumerate(pieces[:-1]):
        out[:, n * HALO : (n + 1) * HALO] = piece[...]


def at(base, size, index):
    return base.at[pl.ds(index * size, size)]


def element_force(vector, stencil, coef):
    high = vector.astype(BF16).astype(F32)
    split = jnp.concatenate([high, vector - high], 0).astype(BF16)
    parts = []
    for moved in (shift_lanes(split, -1), split, shift_lanes(split, 1)):
        parts += [moved, moved[: VEC + PAIR]]
    force = jnp.dot(stencil, jnp.concatenate(parts, 0), preferred_element_type=F32)
    sums = []
    for c in range(COMPS):
        total = None
        for n in range(4):
            first = (c * 4 + n) * PAIR
            piece = force[first : first + PAIR] * coef[n * PAIR : (n + 1) * PAIR]
            total = piece if total is None else total + piece
        sums.append(total)
    return sums


def apply_rows(source, coefs, stencil, start, stop, store):
    weights = stencil[...]
    front = iota((PAIR, source.shape[1]), 0) < LAYERS
    forces = {}
    for pair in range(start - 1, stop + 1):
        forces[pair] = element_force(
            at(source, VEC, pair)[...], weights, at(coefs, 4 * PAIR, pair)[...]
        )
        done = pair - 1
        if done >= start:
            sums = []
            for c in range(COMPS):
                swapped = jnp.where(front, forces[pair][c], forces[done - 1][c])
                sums.append(forces[done][c] + pltpu.roll(swapped, LAYERS, 0))
            store(done, sums)
            del forces[done - 1]


def domain_of(own_rows, cols):
    shell = (lax.axis_size("group") - 1) * own_rows
    base = iota((PAIR, 128), 0) // LAYERS + lax.axis_index("group") * own_rows

    def mask(pair):
        offset = pair - 1 - HALO
        live = jnp.logical_and(base >= -offset, base < shell - offset)
        one = jnp.where(live, 1.0, 0.0)
        return jnp.concatenate([one] * (cols // 128), 1)

    return mask


def relax_kernel(*refs, pieces):
    E = refs[:pieces]
    stencil, theta = refs[pieces : pieces + 2]
    r_out, c_out, x_out, lw_out, ut_out = refs[pieces + 2 : pieces + 7]
    XP, CR, XS, SH, VI = refs[pieces + 7 :]
    group, lat, rad = (lax.axis_index(n) for n in ("group", "lat", "rad"))
    lat_count = lax.axis_size("lat")
    rows, _ = E[0].shape[-2:]
    own_rows = rows - 2 * HALO
    cols = XP.shape[1]
    rad_layers = LAYERS // 2
    planes = COMPS * rad_layers

    def block(lb, rb, plane):
        if pieces == 1:
            return E[0][lb * 2 + rb, plane]
        near, far = [
            jnp.where(rad == rb, E[n][plane], E[n + 1][plane]) for n in (0, 2)
        ]
        return jnp.where(lat == lb, near, far)

    for lb in range(lat_count):
        for rb in range(2):
            for k in range(rad_layers):
                layer = rb * rad_layers + k
                for c in range(COMPS):
                    value = block(lb, rb, c * rad_layers + k)
                    for q in range(2):
                        first = (1 - q) * VEC + c * PAIR + q * LAYERS + layer
                        XS[lb, pl.ds(first, rows, VEC), :] = value
                for ref, plane in ((SH, planes + k), (VI, planes + rad_layers + k)):
                    value = block(lb, rb, plane)
                    for q in range(2):
                        first = (1 - q) * PAIR + q * LAYERS + layer
                        ref[lb, pl.ds(first, rows, PAIR), :] = value

    mask = domain_of(own_rows, cols)
    layer8 = iota((PAIR, cols), 0) % LAYERS
    top_layer, last_layer = layer8 == 0, layer8 == LAYERS - 1
    eighth = jnp.concatenate([0.125 / theta[...]] * (cols // 128), 1)

    def corner_means(nodal, scale):
        both = nodal + pltpu.roll(nodal, LAYERS, 0)
        up = jnp.where(last_layer, 0.0, pltpu.roll(both, PAIR - 1, 0))
        down = jnp.where(top_layer, 0.0, pltpu.roll(both, 1, 0))
        result = []
        for side in (both + up, both + down):
            side = scale * side
            for step in (1, -1):
                result.append(side + shift_lanes(side, step))
        return jnp.concatenate(result, 0)

    for pair in range(4, 29):
        domain = mask(pair)
        shear, viscosity, vector = [
            jnp.concatenate([at(ref.at[lb], size, pair)[...] for lb in range(lat_count)], 1)
            for ref, size in ((SH, PAIR), (VI, PAIR), (XS, VEC))
        ]
        ratio = shear / viscosity
        damp = 1.0 / (1.0 + ratio)
        modulus = domain * shear * damp
        relaxed = modulus * ratio * damp
        at(c_out, 4 * PAIR, pair)[...] = corner_means(modulus, eighth)
        at(CR, 4 * PAIR, pair)[...] = corner_means(relaxed, 0.125)
        at(XP, VEC, pair)[...] = vector * jnp.concatenate([domain] * COMPS, 0)

    def store(pair, sums):
        domain = mask(pair)
        at(r_out, VEC, pair)[...] = jnp.concatenate([-domain * x for x in sums], 0)

    apply_rows(XP, CR, stencil, 5, 28, store)
    for t in range(own_rows // 2):
        x_out[t * VEC : (t + 1) * VEC] = at(XP, VEC, HALO + 1 + 2 * t)[...]

    blocks = lw_out.shape[2] // 3
    map_rows = blocks // 2
    tile_rows = map_rows // lat_count
    row = iota((rows, 1), 0) - HALO + group * own_rows
    shell = (lax.axis_size("group") - 1) * own_rows
    scale = jnp.where(jnp.logical_and(row >= 0, row < shell), -LOAD_SCALE, 0.0)
    own = slice(HALO, HALO + own_rows)
    for lb in range(lat_count):
        table = block(lb, 0, planes + 2 * rad_layers)
        spots = iota((rows, blocks), 1).astype(F32)
        own_spots = iota((own_rows, 128), 1).astype(F32)
        loads = jnp.zeros((rows, blocks), F32)
        lift = jnp.zeros((own_rows, 128), F32)
        for k in range(4):
            index, weight = table[:, k : k + 1], table[:, 4 + k : 5 + k]
            loads = loads + jnp.where(spots == index, weight, 0.0)
            right = index[own] >= map_rows
            near = index[own] - jnp.where(right, map_rows, 0) - (lat * tile_rows).astype(F32)
            here = jnp.logical_and(near >= 0, near < tile_rows)
            mine = jnp.where(right, 1.0, 0.0) == rad.astype(F32)
            spot = jnp.where(jnp.logical_and(here, mine), near, -1.0)
            lift = lift + jnp.where(own_spots == spot, weight[own], 0.0)
        loads = loads * scale
        high = loads.astype(BF16).astype(F32)
        middle = (loads - high).astype(BF16).astype(F32)
        low = loads - high - middle
        lw_out[lb] = jnp.concatenate([high, middle, low], 1).astype(BF16)
        lift = lift * (1.0 / LAYERS)
        for layer in range(LAYERS):
            first = lb * own_rows * LAYERS + layer
            ut_out[pl.ds(first, own_rows, LAYERS), :] = lift


def krylov_kernel(*refs, loads):
    load_refs = refs[:loads]
    stencil, r_in, coefs, x_own, lw, ut = refs[loads : loads + 6]
    payload, v_out = refs[loads + 6 : loads + 8]
    V, TOP = refs[loads + 8 :]
    lat = lax.axis_index("lat")
    lat_count = lax.axis_size("lat")
    cols = r_in.shape[1]
    width = cols // lat_count
    pairs = x_own.shape[0] // VEC
    own_rows = 2 * pairs
    if loads == 2:
        own, other = load_refs[0][...], load_refs[1][...]
        own, other = own.astype(F32), other.astype(F32)
        tiles = [jnp.where(lat == 0, own, other), jnp.where(lat == 0, other, own)]
        field = jnp.concatenate(tiles, 0)
    else:
        field = load_refs[0][...].astype(F32)
    half = field.shape[1] // 2
    blocks = jnp.concatenate([field[:, :half], field[:, half:]], 0)
    blocks = jnp.concatenate([blocks] * 3, 0).astype(BF16)
    for lb in range(lat_count):
        TOP[lb] = jnp.zeros(TOP.shape[1:], F32)
        top = jnp.dot(lw[lb], blocks, preferred_element_type=F32)
        for q in range(2):
            TOP[lb, pl.ds((1 - q) * PAIR + q * LAYERS, top.shape[0], PAIR), :] = top
    for pair in range(5, 28):
        vector = at(r_in, VEC, pair)[...]
        top = [at(TOP.at[lb], PAIR, pair)[...] for lb in range(lat_count)]
        upright = vector[2 * PAIR :] + jnp.concatenate(top, 1)
        at(V.at[0], VEC, pair)[...] = jnp.concatenate([vector[: 2 * PAIR], upright], 0)
    mask = domain_of(own_rows, cols)
    for n in range(ITERS):

        def store(pair, sums, n=n):
            domain = mask(pair)
            fresh = jnp.concatenate([domain * x for x in sums], 0)
            at(V.at[n + 1], VEC, pair)[...] = fresh - at(V.at[n], VEC, pair)[...]

        apply_rows(V.at[n], coefs, stencil, 6 + n, 27 - n, store)

    own_pairs = [HALO + 1 + 2 * t for t in range(pairs)]
    sums = [None] * (2 * ITERS)
    for pair in own_pairs:
        values = [at(V.at[n], VEC, pair)[...] for n in range(ITERS + 1)]
        for k in range(2 * ITERS):
            product = values[k // 2] * values[(k + 1) // 2]
            for r in range(COMPS):
                for c in range(cols // 128):
                    piece = product[PAIR * r : PAIR * r + PAIR, 128 * c : 128 * c + 128]
                    sums[k] = piece if sums[k] is None else sums[k] + piece
    for k in range(2 * ITERS):
        payload[k : k + 1] = jnp.sum(sums[k], 0, keepdims=True)
    fields = []
    upright = slice(2 * PAIR, VEC)
    for lb in range(lat_count):
        lanes = slice(lb * width, (lb + 1) * width)
        row = [[x_own[t * VEC + 2 * PAIR : (t + 1) * VEC, lanes] for t in range(pairs)]]
        for n in range(ITERS):
            row.append([at(V.at[n], VEC, pair)[upright, lanes] for pair in own_pairs])
        fields.append(jnp.concatenate([jnp.concatenate(x, 0) for x in row], 1))
    fields = jnp.concatenate(fields, 0)
    spots = (payload.shape[0] - 2 * ITERS) // (ITERS + 1)
    lift = lax.dot_general(
        ut[:, :spots],
        fields,
        (((0,), (0,)), ((), ())),
        precision=lax.Precision.HIGHEST,
        preferred_element_type=F32,
    )
    for n in range(ITERS + 1):
        payload[2 * ITERS + n * spots : 2 * ITERS + (n + 1) * spots] = lift[
            :, n * width : (n + 1) * width
        ]
    own = pl.ds(pl.multiple_of(lat * width, 128), width)
    for n in range(ITERS):
        for t, pair in enumerate(own_pairs):
            v_out[n, t * VEC : (t + 1) * VEC] = V[n, pair * VEC : (pair + 1) * VEC, own]
    v_out[ITERS] = x_own[:, own]


def scalar_kernel(payload, theta, gamma, lift_out):
    moment = [
        jnp.broadcast_to(jnp.sum(payload[k : k + 1], 1, keepdims=True), (8, 128))
        for k in range(2 * ITERS)
    ]

    def product(left, right, size=False):
        by_degree = {}
        for i, a in enumerate(left):
            for j, b in enumerate(right):
                term = a * b
                if size:
                    term = jnp.abs(term)
                by_degree[i + j] = by_degree[i + j] + term if i + j in by_degree else term
        total = None
        for k, weight in by_degree.items():
            term = weight * (jnp.abs(moment[k]) if size else moment[k])
            total = term if total is None else total + term
        return total

    def shifted(poly):
        result = list(poly) + [jnp.zeros((8, 128), F32)]
        for i, a in enumerate(poly):
            result[i + 1] = result[i + 1] + a
        return result

    one, zero = jnp.ones((8, 128), F32), jnp.zeros((8, 128), F32)
    residual, direction, answer = [one], [one], [zero] * ITERS
    norm = moment[0]
    live = None
    for n in range(ITERS):
        image = shifted(direction)
        step = norm / product(direction, image)
        if live is not None:
            step = jnp.where(live, step, 0.0)
        for i, a in enumerate(direction):
            answer[i] = answer[i] + step * a
        if n == ITERS - 1:
            break
        residual = [
            (residual[i] if i < len(residual) else zero) - step * a for i, a in enumerate(image)
        ]
        fresh = product(residual, residual)
        above = fresh > 1e-7 * product(residual, residual, True)
        live = above if live is None else jnp.logical_and(live, above)
        ratio = jnp.where(live, fresh / norm, 0.0)
        direction = [
            a + (ratio * direction[i] if i < len(direction) else zero)
            for i, a in enumerate(residual)
        ]
        norm = jnp.where(live, fresh, 1.0)
    answer = [a / theta[...] for a in answer]
    for n in range(ITERS):
        gamma[n * 8 : (n + 1) * 8] = answer[n]
    rows = lift_out.shape[0]
    base = 2 * ITERS
    lift = payload[base : base + rows]
    for n in range(ITERS):
        first = base + (n + 1) * rows
        lift = lift + answer[n][0:1] * payload[first : first + rows]
    lift_out[...] = lift


def finish_kernel(gamma, v, disp_out, X):
    rad = lax.axis_index("rad")
    total = v[ITERS]
    for n in range(ITERS):
        total = total + gamma[n * 8 : n * 8 + 1] * v[n]
    X[...] = total
    layers = disp_out.shape[1]
    pairs = disp_out.shape[2] // 2
    for c in range(COMPS):
        for k in range(layers):
            for q in range(2):
                lower = X[pl.ds(c * PAIR + q * LAYERS + k, pairs, VEC), :]
                upper = X[pl.ds(c * PAIR + q * LAYERS + layers + k, pairs, VEC), :]
                disp_out[c, k, pl.ds(q, pairs, 2), :] = jnp.where(rad == 0, lower, upper)


def bed_kernel(own, other, bed, bed_out):
    rad = lax.axis_index("rad")
    half = bed.shape[1] // 2
    for h in range(2):
        lanes = slice(h * half, (h + 1) * half)
        lift = jnp.where(rad == h, own[...], other[...])
        bed_out[:, lanes] = bed[:, lanes] + UPLIFT_SCALE * lift


def per_device(
    displacement_prev,
    shear_modulus,
    viscosity,
    element_matrix,
    regrid_index,
    regrid_weight,
    ice_thickness,
    bed_elevation,
    basal_friction,
    ice_mask,
    speed_guess,
):
    groups, lats = lax.axis_size("group"), lax.axis_size("lat")
    rad_layers, own_rows, width = shear_modulus.shape
    tile_rows, map_cols = ice_thickness.shape
    cols = lats * width
    blocks = 2 * tile_rows * lats
    planes = COMPS * rad_layers + 2 * rad_layers + 1
    ice_args = (speed_guess, ice_thickness, bed_elevation, basal_friction, ice_mask)

    levels = speed_guess.shape[0]
    low, high, *kept = call(
        functools.partial(pack_kernel, map_rows=tile_rows * lats, masked=lats != 2),
        (pltpu.VMEM((planes, HALO, width), F32),) * 2
        + (pltpu.VMEM(speed_guess.shape, F32),)
        + (pltpu.VMEM((tile_rows, map_cols), F32),) * 4
        + (pltpu.VMEM(((levels + 8) * HALO, map_cols), BF16),) * (1 if lats == 2 else 2),
        leave(
            *ice_args,
            displacement_prev,
            shear_modulus,
            viscosity,
            regrid_index[:, 0].T,
            regrid_weight[:, 0].T,
        ),
        [pltpu.VMEM((8, 128), F32)],
    )
    ice_args, edges = kept[:5], kept[5:]
    bed_kept = ice_args[2]
    north = lax.ppermute(high, "group", [(i, (i + 1) % groups) for i in range(groups)])
    south = lax.ppermute(low, "group", [(i, (i - 1) % groups) for i in range(groups)])
    if lats == 2:
        halos = [lax.ppermute(edges[0], "lat", [(0, 1), (1, 0)])]
    else:
        halos = [
            lax.ppermute(edges[1], "lat", [(i, i + 1) for i in range(lats - 1)]),
            lax.ppermute(edges[0], "lat", [(i + 1, i) for i in range(lats - 1)]),
        ]
    stencil, theta = stencil_of(element_matrix)
    north, south, halos, stencil, theta = lax.optimization_barrier(
        (north, south, halos, stencil, theta)
    )
    region = call(
        region_kernel,
        pltpu.VMEM((planes, 2 * own_rows, width), F32),
        keep(north, low, high, south),
    )
    if lats == 2:
        far = lax.ppermute(region, "lat", [(0, 1), (1, 0)])
        ice_load = ice_load_of(*ice_args, halos)
        region, _ = lax.optimization_barrier((region, ice_load))
        near = lax.ppermute(region, "rad", [(0, 1), (1, 0)])
        far, _ = lax.optimization_barrier((far, ice_load))
        pieces = [region, near, far, lax.ppermute(far, "rad", [(0, 1), (1, 0)])]
    else:
        pieces = [lax.all_gather(region, ("lat", "rad"))]
        ice_load = ice_load_of(*ice_args, halos)
    if lats == 2:
        loads = [ice_load, lax.ppermute(ice_load, "lat", [(0, 1), (1, 0)])]
    else:
        loads = [lax.all_gather(ice_load, "lat", axis=0, tiled=True)]
    pairs = own_rows // 2
    r_start, coefs, x_own, lw, ut = call(
        functools.partial(relax_kernel, pieces=len(pieces)),
        (
            pltpu.VMEM((33 * VEC, cols), F32),
            pltpu.VMEM((33 * 4 * PAIR, cols), F32),
            pltpu.VMEM((pairs * VEC, cols), F32),
            pltpu.VMEM((lats, 2 * own_rows, 3 * blocks), BF16),
            pltpu.VMEM((lats * own_rows * LAYERS, 128), F32),
        ),
        keep(*pieces, stencil, theta),
        [
            pltpu.VMEM((33 * VEC, cols), F32),
            pltpu.VMEM((33 * 4 * PAIR, cols), F32),
            pltpu.VMEM((lats, 33 * VEC, width), F32),
            pltpu.VMEM((lats, 33 * PAIR, width), F32),
            pltpu.VMEM((lats, 33 * PAIR, width), F32),
        ],
    )
    spots = tile_rows
    payload, vectors = call(
        functools.partial(krylov_kernel, loads=len(loads)),
        (
            pltpu.VMEM((2 * ITERS + (ITERS + 1) * spots, width), F32),
            pltpu.VMEM((ITERS + 1, pairs * VEC, width), F32),
        ),
        keep(*loads, stencil, r_start, coefs, x_own, lw, ut),
        [
            pltpu.VMEM((ITERS + 1, 33 * VEC, cols), F32),
            pltpu.VMEM((lats, 33 * PAIR, width), F32),
        ],
    )
    step = 1
    while step < groups:
        payload = payload + lax.ppermute(
            payload, "group", [(i, i ^ step) for i in range(groups)]
        )
        step *= 2
    gamma, lift = call(
        scalar_kernel,
        (pltpu.VMEM((8 * ITERS, 128), F32), pltpu.VMEM((tile_rows, width), F32)),
        keep(payload, theta),
    )
    other = lax.ppermute(lift, "rad", [(0, 1), (1, 0)])
    displacement = call(
        finish_kernel,
        jax.ShapeDtypeStruct((COMPS, rad_layers, own_rows, width), F32),
        keep(gamma, vectors),
        [pltpu.VMEM((pairs * VEC, width), F32)],
    )
    bed_new = call(
        bed_kernel,
        jax.ShapeDtypeStruct((tile_rows, map_cols), F32),
        keep(lift, other, bed_kept),
    )
    return displacement, bed_new


def solution(mesh):
    in_specs = (
        P(None, "rad", "group", "lat"),
        P("rad", "group", "lat"),
        P("rad", "group", "lat"),
        P(),
        P("group", "lat", None),
        P("group", "lat", None),
        P("lat", None),
        P("lat", None),
        P("lat", None),
        P("lat", None),
        P(None, "lat", None),
    )
    out_specs = (P(None, "rad", "group", "lat"), P("lat", None))

    return jax.shard_map(
        per_device, mesh=mesh, in_specs=in_specs, out_specs=out_specs, check_vma=False
    )
```

```python
import functools

import jax
import jax.numpy as jnp
import numpy as np
from jax import lax
from jax.experimental import pallas as pl
from jax.experimental.pallas import tpu as pltpu
from jax.sharding import PartitionSpec as P

SWEEPS = 6
ITERS = 4
HALO = 8
COMPS = 3
LAYERS = 4
PAIR = 2 * LAYERS
VEC = COMPS * PAIR
LOAD_SCALE = 20.0
UPLIFT_SCALE = 0.5
ASPECT = 0.01
STRAIN_FLOOR = 0.01
LOW_MODULUS = 0.47

F32 = jnp.float32
BF16 = jnp.bfloat16


def vmem():
    return pl.BlockSpec(memory_space=pltpu.VMEM)


def keep(*arrays):
    return [pltpu.with_memory_space_constraint(a, pltpu.VMEM) for a in arrays]


def leave(*arrays):
    return [pltpu.with_memory_space_constraint(a, pltpu.HBM) for a in arrays]


def call(body, out, inputs, scratch=(), specs=None):
    lats = lax.axis_size("lat")
    return pl.pallas_call(
        body,
        out_shape=out,
        in_specs=specs or [vmem()] * len(inputs),
        out_specs=jax.tree.map(lambda _: vmem(), out),
        scratch_shapes=list(scratch),
        compiler_params=pltpu.CompilerParams(vmem_limit_bytes=(8 if lats == 2 else 40) << 20),
    )(*inputs)


def iota(shape, dim):
    return lax.broadcasted_iota(jnp.int32, shape, dim)


def shift_lanes(x, step):
    zero = jnp.zeros((x.shape[0], 1), x.dtype)
    if step == 1:
        return jnp.concatenate([x[:, 1:], zero], 1)
    return jnp.concatenate([zero, x[:, :-1]], 1)


def ice_kernel(*refs, masked):
    if masked:
        speed, thick, bed, fric, mask, before, after, out, S, PL, ST, RH = refs
    else:
        speed, thick, bed, fric, mask, halo, out, S, PL, ST, RH = refs
    levels, own_rows, cols = speed.shape
    lat = lax.axis_index("lat")
    window = ST.shape[1]
    S[:, 0:HALO, :] = jnp.zeros((levels, HALO, cols), F32)
    S[:, HALO + window :, :] = jnp.zeros((levels, HALO, cols), F32)
    PL[:, 0:HALO, :] = jnp.zeros((5, HALO, cols), F32)
    PL[:, HALO + window :, :] = jnp.zeros((5, HALO, cols), F32)

    def place(start, speeds, four):
        rows = pl.ds(pl.multiple_of(HALO + start, 8), speeds.shape[1])
        S[:, rows, :] = speeds
        for n in range(4):
            PL[n, rows, :] = four[n]

    own_four = [thick[...], bed[...], fric[...], mask[...]]
    if masked:
        own_at = HALO
        place(own_at, speed[...], own_four)
        place(0, *read_edge(before, levels))
        place(HALO + own_rows, *read_edge(after, levels))
    else:
        own_at = lat * HALO
        place(own_at, speed[...], own_four)
        place((1 - lat) * own_rows, *read_edge(halo, levels))
    tiles = range(window // 8)

    def rows_of(t):
        return slice(HALO + 8 * t, HALO + 8 * t + 8)

    sub = iota((8, cols), 0)
    top_row, bottom_row = sub == 0, sub == 7

    def north_of(ref, t, here):
        joined = jnp.where(top_row, ref[rows_of(t + 1)], here)
        return pltpu.roll(joined, 7, 0)

    def south_of(ref, t, here):
        joined = jnp.where(bottom_row, ref[rows_of(t - 1)], here)
        return pltpu.roll(joined, 1, 0)

    factor = 0.5 * 0.25 ** (-1.0 / 3.0)
    PL[4, HALO : HALO + window] = (
        PL[0, HALO : HALO + window] + PL[1, HALO : HALO + window]
    )
    for t in tiles:
        here = PL[4, rows_of(t)]
        PL[1, rows_of(t)] = (
            (-0.5 / factor)
            * PL[3, rows_of(t)]
            * PL[0, rows_of(t)]
            * (north_of(PL.at[4], t, here) - south_of(PL.at[4], t, here))
        )
        PL[2, rows_of(t)] = PL[2, rows_of(t)] * (1.0 / factor)
    if masked:
        count = lax.axis_size("lat")

        def inside(t):
            row = iota((8, cols), 0) + (8 * t - HALO)
            top = jnp.where(lat == 0, 0, -HALO)
            end = jnp.where(lat == count - 1, own_rows, own_rows + HALO)
            return jnp.logical_and(row >= top, row < end)

    def inverse_of(t):
        thickness = PL[0, rows_of(t)]
        if masked:
            thickness = jnp.where(inside(t), thickness, 1.0)
        return (levels - 1) / thickness

    def sweep(_, carry):
        for t in tiles:
            inverse = 0.5 * inverse_of(t)
            driving = PL[1, rows_of(t)]
            for k in range(levels):
                here = S[k, rows_of(t)]
                north, south = north_of(S.at[k], t, here), south_of(S.at[k], t, here)
                east, west = shift_lanes(here, 1), shift_lanes(here, -1)
                above = S[min(k + 1, levels - 1), rows_of(t)]
                below = S[max(k - 1, 0), rows_of(t)]
                by_level = (above - below) * inverse
                if k in (0, levels - 1):
                    by_level = 2.0 * by_level
                by_row = north - south
                by_col = east - west
                strain = (by_row * by_row + 4.0 * STRAIN_FLOOR) + (
                    0.25 * (by_col * by_col) + by_level * by_level
                )
                stiffness = jnp.exp2(jnp.log2(strain) * (-1.0 / 3.0))
                ST[k, 8 * t : 8 * t + 8] = stiffness
                RH[k, 8 * t : 8 * t + 8] = driving + stiffness * (
                    (north + south) + (east + west)
                )
        scale = [(0.5 * ASPECT) * inverse_of(t) * inverse_of(t) for t in tiles]
        value, vertical, stiff, rest = {}, {}, {}, {}
        for k in range(levels):
            for t in tiles:
                rows = slice(8 * t, 8 * t + 8)
                current = ST[0, rows] if k == 0 else stiff[t]
                partial = 4.0 * current
                right = RH[k, rows]
                if k == 0:
                    partial = partial + PL[2, rows_of(t)]
                else:
                    partial = partial + vertical[t] * rest[t]
                    right = right + vertical[t] * value[t]
                diagonal = partial
                if k < levels - 1:
                    stiff[t] = ST[k + 1, rows]
                    vertical[t] = scale[t] * (current + stiff[t])
                    diagonal = partial + vertical[t]
                invert = 1.0 / diagonal
                value[t] = right * invert
                RH[k, rows] = value[t]
                if k < levels - 1:
                    rest[t] = partial * invert
                    ST[k, rows] = vertical[t] * invert
        for k in range(levels - 1, -1, -1):
            for t in tiles:
                rows = slice(8 * t, 8 * t + 8)
                if k < levels - 1:
                    value[t] = RH[k, rows] + ST[k, rows] * value[t]
                fresh = value[t]
                if masked:
                    fresh = jnp.where(inside(t), fresh, 0.0)
                    value[t] = fresh
                S[k, rows_of(t)] = fresh
        return carry

    lax.fori_loop(0, SWEEPS, sweep, 0)
    for t in tiles:
        total = S[0, rows_of(t)]
        for k in range(1, levels):
            total = total + S[k, rows_of(t)]
        PL[4, rows_of(t)] = PL[0, rows_of(t)] * total * (1.0 / levels)
    for t in tiles:
        here = PL[4, rows_of(t)]
        change = north_of(PL.at[4], t, here) - south_of(PL.at[4], t, here)
        fresh = PL[0, rows_of(t)] - 0.25 * change
        PL[1, rows_of(t)] = PL[3, rows_of(t)] * fresh
    out[...] = PL[1, pl.ds(pl.multiple_of(HALO + own_at, 8), own_rows), :].astype(BF16)


def edge_rows(start, speed, thick, bed, fric, mask):
    levels, _, cols = speed.shape
    rows = pl.ds(start if isinstance(start, int) else pl.multiple_of(start, 8), HALO)
    parts = [speed[:, rows, :].reshape(levels * HALO, cols)]
    parts += [plane[rows, :] for plane in (thick, bed, fric)]
    return jnp.concatenate(parts + [mask[rows, :].astype(F32)], 0)


def read_edge(halo, levels):
    value = halo[...]
    four = [value[(levels + n) * HALO : (levels + n + 1) * HALO] for n in range(4)]
    return value[: levels * HALO].reshape(levels, HALO, value.shape[1]), four


def ice_load_of(speed, thick, bed, fric, mask, halos):
    levels, own_rows, cols = speed.shape
    window = own_rows + HALO * (1 if len(halos) == 1 else 2)
    return call(
        functools.partial(ice_kernel, masked=len(halos) != 1),
        pltpu.VMEM((own_rows, cols), BF16),
        keep(speed, thick, bed, fric, mask, *halos),
        [
            pltpu.VMEM((levels, window + 2 * HALO, cols), F32),
            pltpu.VMEM((5, window + 2 * HALO, cols), F32),
            pltpu.VMEM((levels, window, cols), F32),
            pltpu.VMEM((levels, window, cols), F32),
        ],
    )


def stencil_tables():
    pick_row = np.zeros((32 * COMPS, 24), np.float32)
    pick_col = np.zeros((4, 24, 3 * VEC), np.float32)
    keep = np.zeros((4, 32 * COMPS, 3 * VEC), np.float32)
    for c in range(COMPS):
        for p in range(2):
            for s in range(2):
                for q in range(2):
                    for layer in range(LAYERS):
                        m = ((c * 2 + p) * 2 + s) * PAIR + q * LAYERS + layer
                        pick_row[m, 3 * (4 * p + 2 * q + s) + c] = 1.0
                        for dj in range(3):
                            for c2 in range(COMPS):
                                for q2 in range(2):
                                    for l2 in range(LAYERS):
                                        n = dj * VEC + c2 * PAIR + q2 * LAYERS + l2
                                        p2 = l2 - layer + p
                                        s2 = dj - 1 + s
                                        if p2 in (0, 1) and s2 in (0, 1):
                                            keep[2 * p2 + s2, m, n] = 1.0
    for p2 in range(2):
        for s2 in range(2):
            for dj in range(3):
                for c2 in range(COMPS):
                    for q2 in range(2):
                        for l2 in range(LAYERS):
                            n = dj * VEC + c2 * PAIR + q2 * LAYERS + l2
                            pick_col[2 * p2 + s2, 3 * (4 * p2 + 2 * q2 + s2) + c2, n] = 1.0
    return pick_row, pick_col, keep


def stencil_kernel(matrix, pick_row, pick_col, keep, out, theta):
    exact = functools.partial(
        jnp.dot, precision=lax.Precision.HIGHEST, preferred_element_type=F32
    )
    entries = matrix[...]
    rows = exact(pick_row[...], entries)
    full = jnp.zeros((rows.shape[0], 3 * VEC), F32)
    for n in range(4):
        full = full + keep[n] * exact(rows, pick_col[n])
    high = full.astype(BF16).astype(F32)
    low = full - high
    blank = jnp.zeros((rows.shape[0], PAIR), F32)
    parts = []
    for dj in range(3):
        cut = slice(dj * VEC, (dj + 1) * VEC)
        parts += [high[:, cut], high[:, cut], low[:, cut], blank]
    out[...] = jnp.concatenate(parts, 1).astype(BF16)
    square = iota(entries.shape, 0) == iota(entries.shape, 1)
    trace = jnp.sum(jnp.where(square, entries, 0.0), keepdims=True)
    theta[...] = jnp.broadcast_to(trace * (8.0 * LOW_MODULUS / 24.0), (8, 128))


def stencil_of(matrix):
    tables = [jnp.asarray(t) for t in stencil_tables()]
    return call(
        stencil_kernel,
        (
            pltpu.VMEM((32 * COMPS, 3 * (3 * VEC + PAIR)), BF16),
            pltpu.VMEM((8, 128), F32),
        ),
        leave(matrix, *tables),
    )


def pack_kernel(*refs, map_rows, masked):
    ice, (disp, shear, visc, index, weight) = refs[:5], refs[5:10]
    low, high = refs[10:12]
    copies = refs[12:17]
    edges, TS = refs[17:-1], refs[-1]
    for source, copy in zip(ice, copies):
        copy[...] = source[...].astype(F32)
    layers = shear.shape[0]
    count = COMPS * layers
    spot = index[...]
    TS[0:4, 0 : 2 * HALO] = ((spot % 2) * map_rows + spot // 2).astype(F32)
    TS[4:8, 0 : 2 * HALO] = weight[...]
    table = jnp.transpose(TS[...])
    for n, out in enumerate((low, high)):
        rows = slice(n * HALO, (n + 1) * HALO)
        for c in range(COMPS):
            for k in range(layers):
                out[c * layers + k] = disp[c, k, rows]
        for k in range(layers):
            out[count + k] = shear[k, rows]
            out[count + layers + k] = visc[k, rows]
        out[count + 2 * layers, :, 0:8] = table[rows]
    top = ice[0].shape[1] - HALO
    if masked:
        edges[0][...] = edge_rows(0, *ice)
        edges[1][...] = edge_rows(top, *ice)
    else:
        edges[0][...] = edge_rows(jnp.where(lax.axis_index("lat") == 0, top, 0), *ice)


def region_kernel(*pieces):
    out = pieces[-1]
    for n, piece in enumerate(pieces[:-1]):
        out[:, n * HALO : (n + 1) * HALO] = piece[...]


def at(base, size, index):
    return base.at[pl.ds(index * size, size)]


def element_force(vector, stencil, coef):
    high = vector.astype(BF16).astype(F32)
    split = jnp.concatenate([high, vector - high], 0).astype(BF16)
    parts = []
    for moved in (shift_lanes(split, -1), split, shift_lanes(split, 1)):
        parts += [moved, moved[: VEC + PAIR]]
    force = jnp.dot(stencil, jnp.concatenate(parts, 0), preferred_element_type=F32)
    sums = []
    for c in range(COMPS):
        total = None
        for n in range(4):
            first = (c * 4 + n) * PAIR
            piece = force[first : first + PAIR] * coef[n * PAIR : (n + 1) * PAIR]
            total = piece if total is None else total + piece
        sums.append(total)
    return sums


def apply_rows(source, coefs, stencil, start, stop, store):
    weights = stencil[...]
    front = iota((PAIR, source.shape[1]), 0) < LAYERS
    forces = {}
    for pair in range(start - 1, stop + 1):
        forces[pair] = element_force(
            at(source, VEC, pair)[...], weights, at(coefs, 4 * PAIR, pair)[...]
        )
        done = pair - 1
        if done >= start:
            sums = []
            for c in range(COMPS):
                swapped = jnp.where(front, forces[pair][c], forces[done - 1][c])
                sums.append(forces[done][c] + pltpu.roll(swapped, LAYERS, 0))
            store(done, sums)
            del forces[done - 1]


def domain_of(own_rows, cols):
    shell = (lax.axis_size("group") - 1) * own_rows
    base = iota((PAIR, 128), 0) // LAYERS + lax.axis_index("group") * own_rows

    def mask(pair):
        offset = pair - 1 - HALO
        live = jnp.logical_and(base >= -offset, base < shell - offset)
        one = jnp.where(live, 1.0, 0.0)
        return jnp.concatenate([one] * (cols // 128), 1)

    return mask


def relax_kernel(*refs, pieces):
    E = refs[:pieces]
    stencil, theta = refs[pieces : pieces + 2]
    r_out, c_out, x_out, lw_out, ut_out = refs[pieces + 2 : pieces + 7]
    XP, CR, XS, SH, VI = refs[pieces + 7 :]
    group, lat, rad = (lax.axis_index(n) for n in ("group", "lat", "rad"))
    lat_count = lax.axis_size("lat")
    rows, _ = E[0].shape[-2:]
    own_rows = rows - 2 * HALO
    cols = XP.shape[1]
    rad_layers = LAYERS // 2
    planes = COMPS * rad_layers

    def block(lb, rb, plane):
        if pieces == 1:
            return E[0][lb * 2 + rb, plane]
        near, far = [
            jnp.where(rad == rb, E[n][plane], E[n + 1][plane]) for n in (0, 2)
        ]
        return jnp.where(lat == lb, near, far)

    for lb in range(lat_count):
        for rb in range(2):
            for k in range(rad_layers):
                layer = rb * rad_layers + k
                for c in range(COMPS):
                    value = block(lb, rb, c * rad_layers + k)
                    for q in range(2):
                        first = (1 - q) * VEC + c * PAIR + q * LAYERS + layer
                        XS[lb, pl.ds(first, rows, VEC), :] = value
                for ref, plane in ((SH, planes + k), (VI, planes + rad_layers + k)):
                    value = block(lb, rb, plane)
                    for q in range(2):
                        first = (1 - q) * PAIR + q * LAYERS + layer
                        ref[lb, pl.ds(first, rows, PAIR), :] = value

    mask = domain_of(own_rows, cols)
    layer8 = iota((PAIR, cols), 0) % LAYERS
    top_layer, last_layer = layer8 == 0, layer8 == LAYERS - 1
    eighth = jnp.concatenate([0.125 / theta[...]] * (cols // 128), 1)

    def corner_means(nodal, scale):
        both = nodal + pltpu.roll(nodal, LAYERS, 0)
        up = jnp.where(last_layer, 0.0, pltpu.roll(both, PAIR - 1, 0))
        down = jnp.where(top_layer, 0.0, pltpu.roll(both, 1, 0))
        result = []
        for side in (both + up, both + down):
            side = scale * side
            for step in (1, -1):
                result.append(side + shift_lanes(side, step))
        return jnp.concatenate(result, 0)

    for pair in range(4, 29):
        domain = mask(pair)
        shear, viscosity, vector = [
            jnp.concatenate([at(ref.at[lb], size, pair)[...] for lb in range(lat_count)], 1)
            for ref, size in ((SH, PAIR), (VI, PAIR), (XS, VEC))
        ]
        ratio = shear / viscosity
        damp = 1.0 / (1.0 + ratio)
        modulus = domain * shear * damp
        relaxed = modulus * ratio * damp
        four = jnp.concatenate([domain] * 4, 0)
        at(c_out, 4 * PAIR, pair)[...] = four * corner_means(modulus, eighth)
        at(CR, 4 * PAIR, pair)[...] = four * corner_means(relaxed, -0.125)
        at(XP, VEC, pair)[...] = vector * jnp.concatenate([domain] * COMPS, 0)

    def store(pair, sums):
        at(r_out, VEC, pair)[...] = jnp.concatenate(sums, 0)

    apply_rows(XP, CR, stencil, 5, 28, store)
    for t in range(own_rows // 2):
        x_out[t * VEC : (t + 1) * VEC] = at(XP, VEC, HALO + 1 + 2 * t)[...]

    blocks = lw_out.shape[2] // 3
    map_rows = blocks // 2
    tile_rows = map_rows // lat_count
    row = iota((rows, 1), 0) - HALO + group * own_rows
    shell = (lax.axis_size("group") - 1) * own_rows
    scale = jnp.where(jnp.logical_and(row >= 0, row < shell), -LOAD_SCALE, 0.0)
    own = slice(HALO, HALO + own_rows)
    repeats = (own_rows, own_rows * LAYERS)
    spread = jnp.where(iota(repeats, 0) == iota(repeats, 1) // LAYERS, 1.0, 0.0)
    tile_spots = iota((tile_rows, own_rows * LAYERS), 0).astype(F32)
    lifts = []
    for lb in range(lat_count):
        table = block(lb, 0, planes + 2 * rad_layers)
        spots = iota((rows, blocks), 1).astype(F32)
        loads = jnp.zeros((rows, blocks), F32)
        for k in range(4):
            index, weight = table[:, k : k + 1], table[:, 4 + k : 5 + k]
            loads = loads + jnp.where(spots == index, weight, 0.0)
        entries = lax.dot_general(
            table[own][:, 0:8],
            spread,
            (((0,), (0,)), ((), ())),
            precision=lax.Precision.HIGHEST,
            preferred_element_type=F32,
        )
        lift = jnp.zeros((tile_rows, own_rows * LAYERS), F32)
        for k in range(4):
            index, weight = entries[k : k + 1], entries[4 + k : 5 + k]
            spot = index - (lat * tile_rows + rad * map_rows).astype(F32)
            lift = lift + jnp.where(tile_spots == spot, weight, 0.0)
        lifts.append(lift * (1.0 / LAYERS))
        loads = loads * scale
        high = loads.astype(BF16).astype(F32)
        middle = (loads - high).astype(BF16).astype(F32)
        low = loads - high - middle
        lw_out[lb] = jnp.concatenate([high, middle, low], 1).astype(BF16)
    ut_out[...] = jnp.concatenate(lifts, 1)


def krylov_kernel(*refs, loads):
    load_refs = refs[:loads]
    stencil, r_in, coefs, x_own, lw, ut = refs[loads : loads + 6]
    payload, v_out = refs[loads + 6 : loads + 8]
    V, TOP = refs[loads + 8 :]
    lat = lax.axis_index("lat")
    lat_count = lax.axis_size("lat")
    cols = r_in.shape[1]
    width = cols // lat_count
    pairs = x_own.shape[0] // VEC
    if loads == 2:
        own, other = load_refs[0][...], load_refs[1][...]
        own, other = own.astype(F32), other.astype(F32)
        tiles = [jnp.where(lat == 0, own, other), jnp.where(lat == 0, other, own)]
        field = jnp.concatenate(tiles, 0)
    else:
        field = load_refs[0][...].astype(F32)
    half = field.shape[1] // 2
    blocks = jnp.concatenate([field[:, :half], field[:, half:]], 0)
    blocks = jnp.concatenate([blocks] * 3, 0).astype(BF16)
    for lb in range(lat_count):
        TOP[lb] = jnp.zeros(TOP.shape[1:], F32)
        top = jnp.dot(lw[lb], blocks, preferred_element_type=F32)
        for q in range(2):
            TOP[lb, pl.ds((1 - q) * PAIR + q * LAYERS, top.shape[0], PAIR), :] = top
    for pair in range(5, 28):
        vector = at(r_in, VEC, pair)[...]
        top = [at(TOP.at[lb], PAIR, pair)[...] for lb in range(lat_count)]
        upright = vector[2 * PAIR :] + jnp.concatenate(top, 1)
        at(V.at[0], VEC, pair)[...] = jnp.concatenate([vector[: 2 * PAIR], upright], 0)
    for n in range(ITERS):

        def store(pair, sums, n=n):
            fresh = jnp.concatenate(sums, 0) - at(V.at[n], VEC, pair)[...]
            at(V.at[n + 1], VEC, pair)[...] = fresh

        apply_rows(V.at[n], coefs, stencil, 6 + n, 27 - n, store)

    own_pairs = [HALO + 1 + 2 * t for t in range(pairs)]
    sums = [None] * (2 * ITERS)
    for pair in own_pairs:
        values = [at(V.at[n], VEC, pair)[...] for n in range(ITERS + 1)]
        for k in range(2 * ITERS):
            product = values[k // 2] * values[(k + 1) // 2]
            for r in range(COMPS):
                for c in range(cols // 128):
                    piece = product[PAIR * r : PAIR * r + PAIR, 128 * c : 128 * c + 128]
                    sums[k] = piece if sums[k] is None else sums[k] + piece
    for k in range(2 * ITERS):
        payload[k : k + 1] = jnp.sum(sums[k], 0, keepdims=True)
    fields = []
    upright = slice(2 * PAIR, VEC)
    for lb in range(lat_count):
        lanes = slice(lb * width, (lb + 1) * width)
        row = [[x_own[t * VEC + 2 * PAIR : (t + 1) * VEC, lanes] for t in range(pairs)]]
        for n in range(ITERS):
            row.append([at(V.at[n], VEC, pair)[upright, lanes] for pair in own_pairs])
        fields.append(jnp.concatenate([jnp.concatenate(x, 0) for x in row], 1))
    fields = jnp.concatenate(fields, 0)
    spots = (payload.shape[0] - 2 * ITERS) // (ITERS + 1)
    lift = jnp.dot(
        ut[...],
        fields,
        precision=lax.Precision.HIGHEST,
        preferred_element_type=F32,
    )
    for n in range(ITERS + 1):
        payload[2 * ITERS + n * spots : 2 * ITERS + (n + 1) * spots] = lift[
            :, n * width : (n + 1) * width
        ]
    own = pl.ds(pl.multiple_of(lat * width, 128), width)
    for n in range(ITERS):
        for t, pair in enumerate(own_pairs):
            v_out[n, t * VEC : (t + 1) * VEC] = V[n, pair * VEC : (pair + 1) * VEC, own]
    v_out[ITERS] = x_own[:, own]


def scalar_kernel(payload, theta, gamma, lift_out):
    moment = [
        jnp.broadcast_to(jnp.sum(payload[k : k + 1], 1, keepdims=True), (8, 128))
        for k in range(2 * ITERS)
    ]

    def product(left, right, size=False):
        by_degree = {}
        for i, a in enumerate(left):
            for j, b in enumerate(right):
                term = a * b
                if size:
                    term = jnp.abs(term)
                by_degree[i + j] = by_degree[i + j] + term if i + j in by_degree else term
        total = None
        for k, weight in by_degree.items():
            term = weight * (jnp.abs(moment[k]) if size else moment[k])
            total = term if total is None else total + term
        return total

    def shifted(poly):
        result = list(poly) + [jnp.zeros((8, 128), F32)]
        for i, a in enumerate(poly):
            result[i + 1] = result[i + 1] + a
        return result

    one, zero = jnp.ones((8, 128), F32), jnp.zeros((8, 128), F32)
    residual, direction, answer = [one], [one], [zero] * ITERS
    norm = moment[0]
    live = None
    for n in range(ITERS):
        image = shifted(direction)
        step = norm / product(direction, image)
        if live is not None:
            step = jnp.where(live, step, 0.0)
        for i, a in enumerate(direction):
            answer[i] = answer[i] + step * a
        if n == ITERS - 1:
            break
        residual = [
            (residual[i] if i < len(residual) else zero) - step * a for i, a in enumerate(image)
        ]
        fresh = product(residual, residual)
        above = fresh > 1e-7 * product(residual, residual, True)
        live = above if live is None else jnp.logical_and(live, above)
        ratio = jnp.where(live, fresh / norm, 0.0)
        direction = [
            a + (ratio * direction[i] if i < len(direction) else zero)
            for i, a in enumerate(residual)
        ]
        norm = jnp.where(live, fresh, 1.0)
    answer = [a / theta[...] for a in answer]
    for n in range(ITERS):
        gamma[n * 8 : (n + 1) * 8] = answer[n]
    rows = lift_out.shape[0]
    base = 2 * ITERS
    lift = payload[base : base + rows]
    for n in range(ITERS):
        first = base + (n + 1) * rows
        lift = lift + answer[n][0:1] * payload[first : first + rows]
    lift_out[...] = lift


def finish_kernel(gamma, v, disp_out, X):
    rad = lax.axis_index("rad")
    total = v[ITERS]
    for n in range(ITERS):
        total = total + gamma[n * 8 : n * 8 + 1] * v[n]
    X[...] = total
    layers = disp_out.shape[1]
    pairs = disp_out.shape[2] // 2
    for c in range(COMPS):
        for k in range(layers):
            for q in range(2):
                lower = X[pl.ds(c * PAIR + q * LAYERS + k, pairs, VEC), :]
                upper = X[pl.ds(c * PAIR + q * LAYERS + layers + k, pairs, VEC), :]
                disp_out[c, k, pl.ds(q, pairs, 2), :] = jnp.where(rad == 0, lower, upper)


def bed_kernel(own, other, bed, bed_out):
    rad = lax.axis_index("rad")
    half = bed.shape[1] // 2
    for h in range(2):
        lanes = slice(h * half, (h + 1) * half)
        lift = jnp.where(rad == h, own[...], other[...])
        bed_out[:, lanes] = bed[:, lanes] + UPLIFT_SCALE * lift


def per_device(
    displacement_prev,
    shear_modulus,
    viscosity,
    element_matrix,
    regrid_index,
    regrid_weight,
    ice_thickness,
    bed_elevation,
    basal_friction,
    ice_mask,
    speed_guess,
):
    groups, lats = lax.axis_size("group"), lax.axis_size("lat")
    rad_layers, own_rows, width = shear_modulus.shape
    tile_rows, map_cols = ice_thickness.shape
    cols = lats * width
    blocks = 2 * tile_rows * lats
    planes = COMPS * rad_layers + 2 * rad_layers + 1
    ice_args = (speed_guess, ice_thickness, bed_elevation, basal_friction, ice_mask)

    levels = speed_guess.shape[0]
    low, high, *kept = call(
        functools.partial(pack_kernel, map_rows=tile_rows * lats, masked=lats != 2),
        (pltpu.VMEM((planes, HALO, width), F32),) * 2
        + (pltpu.VMEM(speed_guess.shape, F32),)
        + (pltpu.VMEM((tile_rows, map_cols), F32),) * 4
        + (pltpu.VMEM(((levels + 4) * HALO, map_cols), F32),) * (1 if lats == 2 else 2),
        leave(
            *ice_args,
            displacement_prev,
            shear_modulus,
            viscosity,
            regrid_index[:, 0].T,
            regrid_weight[:, 0].T,
        ),
        [pltpu.VMEM((8, 128), F32)],
    )
    ice_args, edges = kept[:5], kept[5:]
    bed_kept = ice_args[2]
    north = lax.ppermute(high, "group", [(i, (i + 1) % groups) for i in range(groups)])
    south = lax.ppermute(low, "group", [(i, (i - 1) % groups) for i in range(groups)])
    if lats == 2:
        halos = [lax.ppermute(edges[0], "lat", [(0, 1), (1, 0)])]
    else:
        halos = [
            lax.ppermute(edges[1], "lat", [(i, i + 1) for i in range(lats - 1)]),
            lax.ppermute(edges[0], "lat", [(i + 1, i) for i in range(lats - 1)]),
        ]
    stencil, theta = stencil_of(element_matrix)
    north, south, halos, stencil, theta = lax.optimization_barrier(
        (north, south, halos, stencil, theta)
    )
    region = call(
        region_kernel,
        pltpu.VMEM((planes, 2 * own_rows, width), F32),
        keep(north, low, high, south),
    )
    if lats == 2:
        far = lax.ppermute(region, "lat", [(0, 1), (1, 0)])
        near = lax.ppermute(region, "rad", [(0, 1), (1, 0)])
        ice_load = ice_load_of(*ice_args, halos)
        far, _ = lax.optimization_barrier((far, ice_load))
        pieces = [region, near, far, lax.ppermute(far, "rad", [(0, 1), (1, 0)])]
    else:
        pieces = [lax.all_gather(region, ("lat", "rad"))]
        ice_load = ice_load_of(*ice_args, halos)
    if lats == 2:
        loads = [ice_load, lax.ppermute(ice_load, "lat", [(0, 1), (1, 0)])]
    else:
        loads = [lax.all_gather(ice_load, "lat", axis=0, tiled=True)]
    pairs = own_rows // 2
    r_start, coefs, x_own, lw, ut = call(
        functools.partial(relax_kernel, pieces=len(pieces)),
        (
            pltpu.VMEM((33 * VEC, cols), F32),
            pltpu.VMEM((33 * 4 * PAIR, cols), F32),
            pltpu.VMEM((pairs * VEC, cols), F32),
            pltpu.VMEM((lats, 2 * own_rows, 3 * blocks), BF16),
            pltpu.VMEM((tile_rows, lats * own_rows * LAYERS), F32),
        ),
        keep(*pieces, stencil, theta),
        [
            pltpu.VMEM((33 * VEC, cols), F32),
            pltpu.VMEM((33 * 4 * PAIR, cols), F32),
            pltpu.VMEM((lats, 33 * VEC, width), F32),
            pltpu.VMEM((lats, 33 * PAIR, width), F32),
            pltpu.VMEM((lats, 33 * PAIR, width), F32),
        ],
    )
    spots = tile_rows
    payload, vectors = call(
        functools.partial(krylov_kernel, loads=len(loads)),
        (
            pltpu.VMEM((2 * ITERS + (ITERS + 1) * spots, width), F32),
            pltpu.VMEM((ITERS + 1, pairs * VEC, width), F32),
        ),
        keep(*loads, stencil, r_start, coefs, x_own, lw, ut),
        [
            pltpu.VMEM((ITERS + 1, 33 * VEC, cols), F32),
            pltpu.VMEM((lats, 33 * PAIR, width), F32),
        ],
    )
    step = 1
    while step < groups:
        payload = payload + lax.ppermute(
            payload, "group", [(i, i ^ step) for i in range(groups)]
        )
        step *= 2
    gamma, lift = call(
        scalar_kernel,
        (pltpu.VMEM((8 * ITERS, 128), F32), pltpu.VMEM((tile_rows, width), F32)),
        keep(payload, theta),
    )
    other = lax.ppermute(lift, "rad", [(0, 1), (1, 0)])
    displacement = call(
        finish_kernel,
        jax.ShapeDtypeStruct((COMPS, rad_layers, own_rows, width), F32),
        keep(gamma, vectors),
        [pltpu.VMEM((pairs * VEC, width), F32)],
    )
    bed_new = call(
        bed_kernel,
        jax.ShapeDtypeStruct((tile_rows, map_cols), F32),
        keep(lift, other, bed_kept),
    )
    return displacement, bed_new


def solution(mesh):
    in_specs = (
        P(None, "rad", "group", "lat"),
        P("rad", "group", "lat"),
        P("rad", "group", "lat"),
        P(),
        P("group", "lat", None),
        P("group", "lat", None),
        P("lat", None),
        P("lat", None),
        P("lat", None),
        P("lat", None),
        P(None, "lat", None),
    )
    out_specs = (P(None, "rad", "group", "lat"), P("lat", None))

    return jax.shard_map(
        per_device, mesh=mesh, in_specs=in_specs, out_specs=out_specs, check_vma=False
    )
```
